128 devices in a mesh: segment: 2 (over x_lo), seq: 16 (over z, y), mp: 4 (over x_hi, core).
Axes of the slice: x: 4 (x_hi: 2, x_lo: 2; x = x_hi * 2 + x_lo), y: 4, z: 4, core: 2. Of those that a mesh axis runs over, the one named last changes fastest.
Arguments:
- memory: bfloat16 [2, 4096, 4096], P(None, 'seq', 'mp')
- decoder_rows: bfloat16 [2, 1024, 4096], P(None, 'seq', 'mp')
- gains: bfloat16 [2, 4096], P('segment'), may hold values from 0.5 to 1.5
- weights: bfloat16 [2, 2, 4096, 4096], P('segment', None, None, 'mp')
- lengths: int32 [2], replicated, may hold values from 512 to 4096, as said below
Outputs:
- decoder_out: bfloat16 [2, 1024, 4096], P(None, 'seq', ('segment', 'mp'))
The draws below stay inside these ranges and needn't reach their ends.
Inputs may be any that keep to these rules, and one draw needn't show every extreme that they name: memory positions of document b at or beyond lengths[b] are padding; some document has all 4096 positions.
All inputs are finite; a program needn't handle non-finite values.
Results may differ from the reference program's by a relative error of at most 0.015.
The reference program's roundings to bfloat16 on the way count: a program that leaves them out, or rounds other values in their place, can miss the bound.
Values may be sent and summed in bfloat16 or wider, within the bound.
A program may use at most 192 MiB of HBM per device.

```python
import math
import jax
import jax.numpy as jnp
from jax import lax

D = 4096
HEADS = 64
DKV = 64
DOCS = 2
HD = 4096
MEM = 4096
LEN = 1024


def draw_both_rows(key):
    rows_key = jax.random.fold_in(key, 17)
    mem_key, dec_key = jax.random.split(rows_key, 2)
    memory = jax.random.normal(mem_key, (DOCS, MEM, D), jnp.float32)
    decoder = jax.random.normal(dec_key, (DOCS, LEN, D), jnp.float32)
    return (memory.astype(jnp.bfloat16), decoder.astype(jnp.bfloat16))


def draw_memory(key, part):
    return draw_both_rows(key)[0]


def draw_decoder_rows(key, part):
    return draw_both_rows(key)[1]


def draw_weights(key, part):
    raw = jax.random.normal(key, (2, 2, D, HD), jnp.float32)
    pair_scale = math.sqrt(3.0 / (D * math.sqrt(DKV)))
    key_weight = raw[0, 0] * pair_scale
    value_weight = raw[0, 1] / math.sqrt(D)
    query_weight = raw[1, 0] * pair_scale
    out_weight = raw[1, 1] * 3.0 / math.sqrt(HD)
    stacked = jnp.stack([jnp.stack([key_weight, value_weight]), jnp.stack([query_weight, out_weight])])
    return stacked.astype(jnp.bfloat16)


def draw_lengths(key, part):
    lowest = max(1, MEM // 8)
    draw_key, full_key = jax.random.split(key)
    drawn = jax.random.randint(draw_key, (DOCS,), lowest, MEM + 1)
    full_doc = jax.random.randint(full_key, (), 0, DOCS)
    return jnp.where(jnp.arange(DOCS) == full_doc, MEM, drawn).astype(jnp.int32)


def setup_inputs(seed: int = 0) -> dict:
    streams_of = jax.random.split(jax.random.key(seed), 6)
    return {
        "memory": draw_memory(jax.random.fold_in(streams_of[5], 71), 0),
        "decoder_rows": draw_decoder_rows(jax.random.fold_in(streams_of[5], 71), 0),
        "gains": jnp.clip(1.0 + 0.1 * jax.random.normal(streams_of[2], (2, D), jnp.float32), 0.5, 1.5).astype(jnp.bfloat16),
        "weights": draw_weights(jax.random.fold_in(streams_of[5], 71), 0),
        "lengths": draw_lengths(jax.random.fold_in(streams_of[5], 71), 0),
    }


norm_eps = 1e-06
masked_score = -1e+30

def rms_rows(rows, gain):
    wide = rows.astype(jnp.float32)
    inverse = lax.rsqrt(lax.optimization_barrier(jnp.mean(wide * wide, axis=-1, keepdims=True)) + norm_eps)
    return (wide * inverse * gain.astype(jnp.float32)[None, :]).astype(jnp.bfloat16)

def one_head(head_inputs):
    query_head, key_head, value_head, valid_keys = head_inputs
    scores = jnp.dot(query_head, key_head.T, preferred_element_type=jnp.float32)
    masked = jnp.where(valid_keys[None, :], scores, masked_score)
    row_max = lax.optimization_barrier(jnp.max(masked, axis=1, keepdims=True))
    exp_scores = jnp.where(valid_keys[None, :], jnp.exp(masked - row_max), 0.0)
    row_total = lax.optimization_barrier(jnp.sum(exp_scores, axis=1, keepdims=True))
    summed = jnp.dot(exp_scores.astype(jnp.bfloat16), value_head, preferred_element_type=jnp.float32)
    return (summed / row_total).astype(jnp.bfloat16)

def one_doc(doc_inputs):
    query_doc, key_doc, value_doc, length = doc_inputs
    valid_keys = jnp.arange(MEM, dtype=jnp.int32) < length
    query_heads = jnp.transpose(query_doc.reshape(LEN, HEADS, DKV), (1, 0, 2))
    key_heads = jnp.transpose(key_doc.reshape(MEM, HEADS, DKV), (1, 0, 2))
    value_heads = jnp.transpose(value_doc.reshape(MEM, HEADS, DKV), (1, 0, 2))
    repeated = jnp.broadcast_to(valid_keys[None, :], (HEADS, MEM))
    context = lax.map(one_head, (query_heads, key_heads, value_heads, repeated))
    return jnp.transpose(context, (1, 0, 2)).reshape(LEN, HD)

def reference(memory, decoder_rows, gains, weights, lengths):
    memory_rows = rms_rows(memory.reshape(DOCS * MEM, D), gains[0])
    target_rows = rms_rows(decoder_rows.reshape(DOCS * LEN, D), gains[1])
    keys = jnp.dot(memory_rows, weights[0, 0], preferred_element_type=jnp.float32).astype(jnp.bfloat16)
    values = jnp.dot(memory_rows, weights[0, 1], preferred_element_type=jnp.float32).astype(jnp.bfloat16)
    queries = jnp.dot(target_rows, weights[1, 0], preferred_element_type=jnp.float32).astype(jnp.bfloat16)
    context = lax.map(one_doc, (queries.reshape(DOCS, LEN, HD), keys.reshape(DOCS, MEM, HD), values.reshape(DOCS, MEM, HD), lengths.astype(jnp.int32)))
    update = lax.dot_general(context.reshape(DOCS * LEN, HD), weights[1, 1], (((1,), (1,)), ((), ())), preferred_element_type=jnp.float32)
    decoder_out = (decoder_rows.reshape(DOCS * LEN, D).astype(jnp.float32) + update).astype(jnp.bfloat16)
    return decoder_out.reshape(DOCS, LEN, D)
```

```python
import jax
import jax.numpy as jnp
from jax import lax
from jax.experimental import pallas as pl
from jax.experimental.pallas import tpu as pltpu
from jax.sharding import PartitionSpec as P

MESH = pl.DeviceIdType.MESH
EPS = 1e-6
MASKED = -1e30
SEQ = 16
GROUP = 8
ROWS = 256


def body(
    mem, dec, gain, w, lens, out,
    wbuf, xf, xd, xn, kvs, kvr, qs, qr, q2, acc, mx, tot, cs, cr, cx, rs, rr, res,
    w_sem, own_sem, ga_s, ga_r, gb_s, gb_r, gc_s, gc_r, kv_s, kv_r, q_s, q_r, c_s, c_r, rs_s, rs_r, res_s, res_r,
):
    s = lax.axis_index("segment")
    q = lax.axis_index("seq")
    m = lax.axis_index("mp")
    across = jnp.bitwise_xor(m, 2)
    beside = jnp.bitwise_xor(m, 1)
    corner = jnp.bitwise_xor(m, 3)
    rot = q // 2
    odd = q % 2
    group = jnp.where(s == 0, m, jnp.where(odd == 0, m, across))
    encoding = s == 0
    decoding = s == 1

    def remote(src, dst, ssem, rsem, device):
        return pltpu.make_async_remote_copy(
            src_ref=src, dst_ref=dst, send_sem=ssem, recv_sem=rsem, device_id=device, device_id_type=MESH
        )

    def kv_weight(j, t):
        return pltpu.make_async_copy(
            w.at[0, t, :, pl.ds(pl.multiple_of(j * 128, 128), 128)],
            wbuf.at[j, :, pl.ds(t * 128, 128)],
            w_sem.at[j, t],
        )

    def dec_weight(t, b):
        return pltpu.make_async_copy(
            w.at[0, t, :, pl.ds(b * 256, 256)], wbuf.at[4 * t + b], w_sem.at[4 * t + b, 0]
        )

    @pl.when(encoding)
    def _():
        for jj in range(8):
            for t in range(2):
                kv_weight(lax.rem(jj + rot, 8), t).start()

    @pl.when(decoding)
    def _():
        for t in range(2):
            for b in range(4):
                dec_weight(t, b).start()

    bar = pltpu.get_barrier_semaphore()

    def greet(k, _):
        for ss in range(2):
            for mm in (m, across):
                pl.semaphore_signal(bar, inc=1, device_id=(ss, k, mm), device_id_type=MESH)
        return 0

    lax.fori_loop(0, SEQ, greet, 0)
    for ss in range(2):
        for mm in (beside, corner):
            pl.semaphore_signal(bar, inc=1, device_id=(ss, q, mm), device_id_type=MESH)
    pl.semaphore_wait(bar, 4 * SEQ + 4)

    def mem_chunk(c):
        return mem.at[:, pl.ds(c * 128, 128), :]

    def own_mem(c):
        return pltpu.make_async_copy(mem_chunk(c), xf.at[m, c], own_sem.at[c])

    def a_mem(c):
        return remote(mem_chunk(c), xf.at[m, c], ga_s.at[c], ga_r.at[c], (0, q, across))

    def a_mem_in(c):
        return remote(mem_chunk(c), xf.at[across, c], ga_s.at[c], ga_r.at[c], (0, q, across))

    def b_mem(c):
        return remote(mem_chunk(c), xf.at[m, c], gb_s.at[c], gb_r.at[c], (0, q, beside))

    def c_mem(c):
        return remote(xf.at[across, c], xf.at[across, c], gc_s.at[c], gc_r.at[c], (0, q, beside))

    own_dec = pltpu.make_async_copy(dec, xd.at[m], own_sem.at[0])
    a_dec = remote(dec, xd.at[m], ga_s.at[0], ga_r.at[0], (1, q, across))
    b_dec = remote(dec, xd.at[m], gb_s.at[0], gb_r.at[0], (1, q, beside))
    c_dec = remote(xd.at[across], xd.at[across], gc_s.at[0], gc_r.at[0], (1, q, beside))

    def normalise(load, rows):
        def step(r, _):
            start = pl.multiple_of(r * 16, 16)
            total = jnp.zeros((16, 1), jnp.float32)
            for k in range(4):
                part = load(k, start).astype(jnp.float32)
                total = total + jnp.sum(part * part, axis=1, keepdims=True)
            inverse = lax.rsqrt(total * (1.0 / 4096) + EPS)
            for k in range(4):
                part = load(k, start).astype(jnp.float32)
                wide = part * inverse * gain[:, k * 1024 : (k + 1) * 1024].astype(jnp.float32)
                xn[pl.ds(start, 16), k * 1024 : (k + 1) * 1024] = wide.astype(jnp.bfloat16)
            return 0

        lax.fori_loop(0, rows // 16, step, 0)

    low = lax.broadcasted_iota(jnp.int32, (1, 128), 1) < 64

    def kv_out(c, i, doc, device):
        return remote(kvs.at[c, i, doc], kvr.at[c, q], kv_s.at[c, i, doc], kv_r.at[c, q], device)

    def unit_of(doc, i, e):
        return (0, i, m) if doc == 0 else (1, i, m if e == 0 else across)

    @pl.when(encoding)
    def _():
        a_dec.start()
        for c in range(2):
            own_mem(c).start()
            b_mem(c).start()
        for c in range(2):
            a_mem_in(c).wait_recv()
            c_mem(c).start()
            own_mem(c).wait()
            b_mem(c).wait_recv()
            c_mem(c).wait_recv()

            def load(k, start, c=c):
                return xf[k, c, start // 128, pl.ds(pl.multiple_of(start % 128, 16), 16), :]

            normalise(load, 256)

            def project(jj, _, c=c):
                j = lax.rem(jj + rot, 8)
                if c == 0:
                    for t in range(2):
                        kv_weight(j, t).wait()
                both = jnp.dot(xn[...], wbuf[j], preferred_element_type=jnp.float32)
                key, value = both[:, :128], both[:, 128:]
                key = pltpu.roll(key, 64, 1)
                for e in range(2):
                    i = 2 * j + e
                    tile = jnp.where(low, value, key) if e == 0 else jnp.where(low, key, value)
                    tile = tile.astype(jnp.bfloat16).reshape(2, 128, 128)
                    kvs[c, i] = tile

                    @pl.when(i == q)
                    def _(tile=tile):
                        kvr[c, q] = tile[0]

                    kv_out(c, i, 1, unit_of(1, i, e)).start()

                    @pl.when(i != q)
                    def _(i=i, e=e):
                        kv_out(c, i, 0, unit_of(0, i, e)).start()

                return 0

            lax.fori_loop(0, 8, project, 0)

    def q_out(i, doc, device):
        return remote(
            qs.at[i // 2, doc], qr.at[q], q_s.at[i, doc], q_r.at[q], device
        )

    residual_out = remote(
        xd.at[m // 2, :, :, pl.ds(pl.multiple_of((m % 2) * 512, 512), 512)], res, res_s, res_r, (0, q, m)
    )

    @pl.when(decoding)
    def _():
        for c in range(2):
            a_mem(c).start()
        own_dec.start()
        b_dec.start()
        remote(dec, xd.at[across], ga_s.at[0], ga_r.at[0], (1, q, across)).wait_recv()
        c_dec.start()
        own_dec.wait()
        b_dec.wait_recv()
        c_dec.wait_recv()
        residual_out.start()

        def load(k, start):
            return xd[k, start // 64, pl.ds(pl.multiple_of(start % 64, 16), 16), :]

        normalise(load, 128)
        for b in range(4):
            dec_weight(0, b).wait()
            made = jnp.dot(xn[:128, :], wbuf[b], preferred_element_type=jnp.float32)
            for u in range(2):
                t = 2 * b + u
                tile = pltpu.roll(made[:, u * 128 : (u + 1) * 128], 64, 1)
                tile = tile.astype(jnp.bfloat16).reshape(2, 64, 128)
                qs[t] = tile
                for e in range(2):
                    i = 2 * t + e
                    q_out(i, 0, unit_of(0, i, e)).start()
                    if e == 1:
                        q_out(i, 1, unit_of(1, i, e)).start()
                    else:

                        @pl.when(q != i)
                        def _(i=i, e=e):
                            q_out(i, 1, unit_of(1, i, e)).start()

                        @pl.when(q == i)
                        def _(tile=tile):
                            qr[q] = tile[1]

    def q_in(k, _):
        @pl.when(jnp.logical_or(encoding, jnp.logical_or(odd == 1, k != q)))
        def _():
            remote(qs.at[0, 0], qr.at[k], q_s.at[0, 0], q_r.at[k], (s, q, m)).wait_recv()

        return 0

    lax.fori_loop(0, SEQ, q_in, 0)
    lane = lax.broadcasted_iota(jnp.int32, (1, 128), 1)
    key_half = jnp.where(odd == 1, 0, 1)
    key_lane = (lane // 64) == key_half
    q2[...] = jnp.where(key_lane, qr[...].reshape(1024, 128), jnp.bfloat16(0))
    mx[...] = jnp.full_like(mx, MASKED)
    tot[...] = jnp.zeros_like(tot)
    acc[...] = jnp.zeros_like(acc)
    length = lens[s]
    span = GROUP * 128

    def attend(step, _):
        c = step // (SEQ // GROUP)
        g = step % (SEQ // GROUP)

        def kv_in(k, _):
            src = g * GROUP + k

            @pl.when(jnp.logical_or(decoding, src != q))
            def _():
                remote(kvs.at[0, 0, 0], kvr.at[c, src], kv_s.at[0, 0, 0], kv_r.at[c, src], (s, q, m)).wait_recv()

            return 0

        lax.fori_loop(0, GROUP, kv_in, 0)
        kv = kvr[c, pl.ds(g * GROUP, GROUP)].reshape(span, 128)
        col = lax.broadcasted_iota(jnp.int32, (1, span), 1)
        position = (g * GROUP + col // 128) * 256 + c * 128 + col % 128
        valid = position < length
        for r in range(1024 // ROWS):
            rows = pl.ds(r * ROWS, ROWS)
            scores = lax.dot_general(
                q2[rows, :], kv, (((1,), (1,)), ((), ())), preferred_element_type=jnp.float32
            )
            scores = jnp.where(valid, scores, MASKED)
            before = mx[rows, :]
            after = jnp.maximum(before, jnp.max(scores, axis=1, keepdims=True))
            probs = jnp.exp(scores - jnp.concatenate([after] * GROUP, axis=1))
            scale = jnp.exp(before - after)
            part = probs[:, :128]
            for k in range(1, GROUP):
                part = part + probs[:, k * 128 : (k + 1) * 128]
            tot[rows, :] = tot[rows, :] * scale + part
            acc[rows, :] = acc[rows, :] * scale + jnp.dot(
                probs.astype(jnp.bfloat16), kv, preferred_element_type=jnp.float32
            )
            mx[rows, :] = after
        return 0

    lax.fori_loop(0, 2 * SEQ // GROUP, attend, 0)

    def c_out(k):
        return remote(cs.at[k], cr.at[s, q], c_s.at[k], c_r.at[s, q], (1, k, group))

    own_context = jnp.logical_and(decoding, odd == 0)

    for k in range(SEQ):
        rows = pl.ds(k * 64, 64)
        total = jnp.sum(tot[rows, :], axis=1, keepdims=True)
        context = jnp.where(key_lane, 0.0, acc[rows, :] / total).astype(jnp.bfloat16)
        cs[k] = context
        mine = jnp.logical_and(own_context, q == k)

        @pl.when(mine)
        def _(context=context):
            cr[1, q] = context

        @pl.when(jnp.logical_not(mine))
        def _(k=k):
            c_out(k).start()

    def rs_out(g):
        return remote(rs.at[g], rr.at[m], rs_s.at[g], rs_r.at[m], (g // 4, q, g % 4))

    @pl.when(decoding)
    def _():
        def c_in(k, _):
            remote(cs.at[0], cr.at[0, k], c_s.at[0], c_r.at[0, k], (s, q, m)).wait_recv()

            @pl.when(jnp.logical_or(odd == 1, k != q))
            def _():
                remote(cs.at[0], cr.at[1, k], c_s.at[0], c_r.at[1, k], (s, q, m)).wait_recv()

            return 0

        lax.fori_loop(0, SEQ, c_in, 0)
        for d in range(2):
            for t in range(8):
                cx[d * 64 : (d + 1) * 64, t * 128 : (t + 1) * 128] = cr[d, 2 * t] + cr[d, 2 * t + 1]
        for b in range(4):
            dec_weight(1, b).wait()

        for g in range(8):
            part = jnp.zeros((128, 512), jnp.float32)
            for b in range(4):
                part = part + lax.dot_general(
                    cx[:, b * 256 : (b + 1) * 256],
                    wbuf[4 + b, g * 512 : (g + 1) * 512, :],
                    (((1,), (1,)), ((), ())),
                    preferred_element_type=jnp.float32,
                )
            rs[g] = part.astype(jnp.bfloat16).reshape(2, 64, 512)
            if g < 4:
                rs_out(g).start()
            else:

                @pl.when(m != g - 4)
                def _(g=g):
                    rs_out(g).start()

                @pl.when(m == g - 4)
                def _(part=part):
                    rr[m] = part.astype(jnp.bfloat16).reshape(2, 64, 512)
                    res[...] = xd[2 + m // 2, :, :, pl.ds(pl.multiple_of((m % 2) * 512, 512), 512)]

    @pl.when(encoding)
    def _():
        residual_out.wait_recv()

    for k in range(4):

        @pl.when(jnp.logical_or(encoding, m != k))
        def _(k=k):
            remote(rs.at[0], rr.at[k], rs_s.at[0], rs_r.at[k], (s, q, m)).wait_recv()

    update = rr[0].astype(jnp.float32)
    for k in range(1, 4):
        update = update + rr[k].astype(jnp.float32)
    out[...] = (res[...].astype(jnp.float32) + update).astype(jnp.bfloat16)

    def c_done(k, _):
        @pl.when(jnp.logical_not(jnp.logical_and(own_context, q == k)))
        def _():
            c_out(k).wait_send()

        return 0

    lax.fori_loop(0, SEQ, c_done, 0)

    @pl.when(encoding)
    def _():
        a_dec.wait_send()
        for c in range(2):
            b_mem(c).wait_send()
            c_mem(c).wait_send()

        def kv_done(i, _):
            for c in range(2):
                kv_out(c, i, 1, (1, q, m)).wait_send()

                @pl.when(i != q)
                def _(c=c):
                    kv_out(c, i, 0, (1, q, m)).wait_send()

            return 0

        lax.fori_loop(0, SEQ, kv_done, 0)

    @pl.when(decoding)
    def _():
        for c in range(2):
            a_mem(c).wait_send()
        b_dec.wait_send()
        c_dec.wait_send()
        residual_out.wait_send()

        def q_done(i, _):
            q_out(i, 0, (0, q, m)).wait_send()

            @pl.when(jnp.logical_or(odd == 1, i != q))
            def _():
                q_out(i, 1, (0, q, m)).wait_send()

            return 0

        lax.fori_loop(0, SEQ, q_done, 0)
        for g in range(8):

            @pl.when(m != g - 4)
            def _(g=g):
                rs_out(g).wait_send()


def on_device(memory, decoder_rows, gains, weights, lengths):
    bf16, f32 = jnp.bfloat16, jnp.float32
    anywhere = pl.BlockSpec(memory_space=pl.ANY)
    vmem = pl.BlockSpec(memory_space=pltpu.VMEM)
    dma = pltpu.SemaphoreType.DMA
    return pl.pallas_call(
        body,
        name="cross_attention",
        out_shape=jax.ShapeDtypeStruct((2, 64, 512), bf16),
        in_specs=[anywhere, anywhere, vmem, anywhere, pl.BlockSpec(memory_space=pltpu.SMEM)],
        out_specs=vmem,
        scratch_shapes=[
            pltpu.VMEM((8, 4096, 256), bf16),
            pltpu.VMEM((4, 2, 2, 128, 1024), bf16),
            pltpu.VMEM((4, 2, 64, 1024), bf16),
            pltpu.VMEM((256, 4096), bf16),
            pltpu.VMEM((2, 16, 2, 128, 128), bf16),
            pltpu.VMEM((2, 16, 128, 128), bf16),
            pltpu.VMEM((8, 2, 64, 128), bf16),
            pltpu.VMEM((16, 64, 128), bf16),
            pltpu.VMEM((1024, 128), bf16),
            pltpu.VMEM((1024, 128), f32),
            pltpu.VMEM((1024, 128), f32),
            pltpu.VMEM((1024, 128), f32),
            pltpu.VMEM((16, 64, 128), bf16),
            pltpu.VMEM((2, 16, 64, 128), bf16),
            pltpu.VMEM((128, 1024), bf16),
            pltpu.VMEM((8, 2, 64, 512), bf16),
            pltpu.VMEM((4, 2, 64, 512), bf16),
            pltpu.VMEM((2, 64, 512), bf16),
            dma((8, 2)),
            dma((2,)),
            dma((2,)),
            dma((2,)),
            dma((2,)),
            dma((2,)),
            dma((2,)),
            dma((2,)),
            dma((2, 16, 2)),
            dma((2, 16)),
            dma((16, 2)),
            dma((16,)),
            dma((16,)),
            dma((2, 16)),
            dma((8,)),
            dma((4,)),
            dma,
            dma,
        ],
        compiler_params=pltpu.CompilerParams(
            collective_id=0, has_side_effects=True, vmem_limit_bytes=56 << 20
        ),
    )(memory, decoder_rows, gains, weights, lengths)


def solution(mesh):
    in_specs = (
        P(None, "seq", "mp"),
        P(None, "seq", "mp"),
        P("segment", None),
        P("segment", None, None, "mp"),
        P(),
    )
    out_specs = P(None, "seq", ("segment", "mp"))
    return jax.shard_map(
        on_device, mesh=mesh, in_specs=in_specs, out_specs=out_specs, check_vma=False
    )
```

```python
import jax
import jax.numpy as jnp
from jax import lax
from jax.experimental import pallas as pl
from jax.experimental.pallas import tpu as pltpu
from jax.sharding import PartitionSpec as P

MESH = pl.DeviceIdType.MESH
EPS = 1e-6
MASKED = -1e30
SEQ = 16
ROWS = 256
SPAN = 2048
PIECE = 16
DIRECT = ((0, 1, 2, 3, 4), (8, 9, 10, 11, 12))
RELAYED = (5, 6, 7, 13, 14, 15)
ARRIVAL = ((0, 1, 2, 5, 3, 6, 4, 7), (8, 9, 10, 13, 11, 14, 12, 15))


def seq_of(n):
    return (n % 4) * 4 + (n // 4 + n % 4) % 4


def body(
    mem, dec, gain, w, lens, out,
    wbuf, wo, xf, xd, relay, xn, kvs, kvr, qs, qr, q2, acc, mx, cs, cr, cx, rs, rr, res,
    w_sem, wo_sem, wx_s, wx_r, own_sem, gp_r, gf_r, fl_s, fw_s, gb_s, gb_r, d_s, d_r,
    kv_s, kv_r, q_s, q_r, c_s, c_r, x_s, x_r, rs_s, rs_r, res_s, res_r,
):
    s = lax.axis_index("segment")
    q = lax.axis_index("seq")
    m = lax.axis_index("mp")
    across = jnp.bitwise_xor(m, 2)
    beside = jnp.bitwise_xor(m, 1)
    half, core = m // 2, m % 2
    z, y = q // 4, q % 4
    slot = 4 * lax.rem(y - z + 4, 4) + z
    odd = z % 2
    group = jnp.where(s == 0, m, jnp.where(odd == 0, m, across))
    encoding = s == 0
    decoding = s == 1

    def remote(src, dst, ssem, rsem, device):
        return pltpu.make_async_remote_copy(
            src_ref=src, dst_ref=dst, send_sem=ssem, recv_sem=rsem, device_id=device, device_id_type=MESH
        )

    def kv_weight(j, t):
        return pltpu.make_async_copy(
            w.at[0, t, :, pl.ds(pl.multiple_of(j * 256, 256), 256)],
            wbuf.at[j, :, pl.ds(t * 256, 256)],
            w_sem,
        )

    def q_weight(b):
        return pltpu.make_async_copy(w.at[0, 0, :, pl.ds(b * 512, 512)], wbuf.at[b], w_sem)

    def out_rows(k, c):
        return w.at[0, 1, pl.ds(pl.multiple_of((2 * k + c) * 512, 512), 512), :]

    def o_weight(k):
        return pltpu.make_async_copy(out_rows(k, core), wo.at[core, k], wo_sem)

    def o_weight_out(k):
        return remote(out_rows(k, 1 - core), wo.at[core, k], wx_s, wx_r, (1, q, beside))

    @pl.when(encoding)
    def _():
        for jj in range(4):
            for t in range(2):
                kv_weight(jj, t).start()

    @pl.when(decoding)
    def _():
        for b in range(2):
            q_weight(b).start()
        for k in range(4):
            o_weight(k).start()

    bar = pltpu.get_barrier_semaphore()

    def hello(*device):
        pl.semaphore_signal(bar, inc=1, device_id=device, device_id_type=MESH)

    def greet(k, _):
        k_odd = (k // 4) % 2 == 1
        hello(0, k, m)

        @pl.when(jnp.logical_or(encoding, jnp.logical_not(jnp.logical_and(k_odd, odd == 1))))
        def _():
            hello(1, k, m)

        @pl.when(jnp.logical_or(k_odd, jnp.logical_and(decoding, jnp.logical_or(odd == 1, k == q))))
        def _():
            hello(1, k, across)

        @pl.when(jnp.logical_and(decoding, jnp.logical_or(odd == 1, k == q)))
        def _():
            hello(0, k, across)

        @pl.when(jnp.logical_and(encoding, jnp.logical_and(odd == 0, k == q)))
        def _():
            hello(1, k, across)

        return 0

    hello(s, q, beside)
    lax.fori_loop(0, SEQ, greet, 0)
    peers = jnp.where(encoding, jnp.where(odd == 1, 41, 42), jnp.where(odd == 1, 57, 43))
    pl.semaphore_wait(bar, peers)

    def piece(ref, p):
        return ref.at[:, pl.ds(p * PIECE, PIECE), :]

    def direct(p):
        return remote(piece(mem, p), piece(xf.at[m], p), fl_s, gp_r.at[p], (0, q, across))

    def hop(n):
        p = RELAYED[n]
        return remote(piece(mem, p), relay.at[n], fl_s, gp_r.at[p], (1, q, across))

    def relayed(n):
        p = RELAYED[n]
        return remote(relay.at[n], piece(xf.at[across], p), fw_s, gp_r.at[p], (0, q, m))

    def piece_in(p):
        return remote(piece(mem, p), piece(xf.at[across], p), fl_s, gp_r.at[p], (0, q, m))

    def forward(p):
        return remote(
            piece(xf.at[across], p), piece(xf.at[across], p), fw_s, gf_r.at[p], (0, q, beside)
        )

    def forward_in(p):
        there = jnp.bitwise_xor(beside, 2)
        return remote(piece(mem, p), piece(xf.at[there], p), fw_s, gf_r.at[p], (0, q, beside))

    def mem_half(c):
        return mem.at[:, pl.ds(c * 128, 128), :]

    own_mem = pltpu.make_async_copy(mem, xf.at[m], own_sem)

    def b_mem(c):
        return remote(
            mem_half(c), xf.at[m, :, pl.ds(c * 128, 128), :], gb_s.at[c], gb_r.at[c], (0, q, beside)
        )

    own_dec = pltpu.make_async_copy(dec, xd.at[m], own_sem)
    a_dec = remote(dec, xd.at[m], d_s.at[0], d_r.at[0], (1, q, across))
    b_dec = remote(dec, xd.at[m], d_s.at[0], d_r.at[1], (1, q, beside))
    c_dec = remote(xd.at[across], xd.at[across], d_s.at[1], d_r.at[2], (1, q, beside))

    def normalise(source, start, put):
        total = jnp.zeros((2, PIECE, 1), jnp.float32)
        for k in range(4):
            part = source[k, :, pl.ds(start, PIECE), :].astype(jnp.float32)
            total = total + jnp.sum(part * part, axis=2, keepdims=True)
        inverse = lax.rsqrt(total * (1.0 / 4096) + EPS)
        for k in range(4):
            part = source[k, :, pl.ds(start, PIECE), :].astype(jnp.float32)
            wide = part * inverse * gain[:, k * 1024 : (k + 1) * 1024].astype(jnp.float32)
            put(slice(k * 1024, (k + 1) * 1024), wide.astype(jnp.bfloat16))

    low = lax.broadcasted_iota(jnp.int32, (1, 128), 1) < 64

    def tile_of(c, i, doc):
        return (c * SEQ + i) * 2 + doc

    def kv_out(c, i, doc, device):
        return remote(kvs.at[tile_of(c, i, doc)], kvr.at[c, q], kv_s, kv_r.at[c], device)

    def unit_of(doc, i, e):
        return (0, seq_of(i), m) if doc == 0 else (1, seq_of(i), m if e % 2 == 0 else across)

    def normalise_mem(p):
        c, at = p // 8, (p % 8) * PIECE

        def put(columns, value):
            xn[c, at : at + PIECE, columns] = value[0]
            xn[c, 128 + at : 128 + at + PIECE, columns] = value[1]

        normalise(xf, p * PIECE, put)

    @pl.when(encoding)
    def _():
        hop(0).start()
        b_mem(0).start()
        for n in range(1, 6):
            hop(n).start()
        a_dec.start()
        own_mem.start()

        def ready(p):
            forward_in(p).wait_recv()
            normalise_mem(p)

        own_mem.wait()
        b_mem(0).wait_recv()
        for n, p in enumerate(ARRIVAL[0]):
            piece_in(p).wait_recv()
            forward(p).start()
            if n >= 2:
                ready(ARRIVAL[0][n - 2])
        b_mem(1).start()
        ready(ARRIVAL[0][6])
        ready(ARRIVAL[0][7])
        pltpu.make_async_copy(wbuf, wbuf, w_sem).wait()

        def project(c, jj):
            j = lax.rem(jj + y, 4)
            both = jnp.dot(xn[c], wbuf[j], preferred_element_type=jnp.float32)
            for u in range(2):
                key = pltpu.roll(both[:, u * 128 : (u + 1) * 128], 64, 1)
                value = both[:, 256 + u * 128 : 256 + (u + 1) * 128]
                for e in range(2):
                    i = 4 * j + 2 * u + e
                    tile = jnp.where(low, value, key) if e == 0 else jnp.where(low, key, value)
                    kvs[pl.ds(tile_of(c, i, 0), 2)] = tile.astype(jnp.bfloat16).reshape(2, 128, 128)
            for e in range(4):
                i = 4 * j + e
                kv_out(c, i, 1, unit_of(1, i, e)).start()

                @pl.when(i != slot)
                def _(i=i, e=e):
                    kv_out(c, i, 0, unit_of(0, i, e)).start()

                @pl.when(i == slot)
                def _(i=i):
                    pltpu.make_async_copy(kvs.at[tile_of(c, i, 0)], kvr.at[c, q], kv_r.at[c]).start()

        waiting = []
        for jj in range(4):
            project(0, jj)
            for p in waiting:
                ready(p)
            waiting = ARRIVAL[1][2 * jj : 2 * jj + 2]
            if jj == 0:
                b_mem(1).wait_recv()
            for p in waiting:
                piece_in(p).wait_recv()
                forward(p).start()
        for p in waiting:
            ready(p)
        for jj in range(4):
            project(1, jj)

    def q_out(i, doc, device):
        return remote(qs.at[i, doc], qr.at[slot], q_s, q_r, device)

    residual_out = remote(
        xd.at[m // 2, :, :, pl.ds(pl.multiple_of((m % 2) * 512, 512), 512)], res, res_s, res_r, (0, q, m)
    )

    @pl.when(decoding)
    def _():
        for p in DIRECT[0]:
            direct(p).start()
        own_dec.start()
        b_dec.start()

        def pass_on(n):
            p = RELAYED[n]
            remote(piece(mem, p), relay.at[n], fl_s, gp_r.at[p], (1, q, across)).wait_recv()
            relayed(n).start()

        for n in range(3):
            pass_on(n)
        for p in DIRECT[1]:
            direct(p).start()
        for n in range(3, 6):
            pass_on(n)
        remote(dec, xd.at[across], d_s.at[0], d_r.at[0], (1, q, across)).wait_recv()
        c_dec.start()
        own_dec.wait()
        b_dec.wait_recv()
        c_dec.wait_recv()
        for p in range(4):

            def put(columns, value, p=p):
                xn[0, p * PIECE : (p + 1) * PIECE, columns] = value[0]
                xn[0, 64 + p * PIECE : 64 + (p + 1) * PIECE, columns] = value[1]

            normalise(xd, p * PIECE, put)
        pltpu.make_async_copy(wbuf.at[0:2], wbuf.at[0:2], w_sem).wait()
        for b in range(2):
            made = jnp.dot(xn[0, :128, :], wbuf[b], preferred_element_type=jnp.float32)
            for u in range(4):
                pair = made[:, u * 128 : (u + 1) * 128]
                turned = pltpu.roll(pair, 64, 1)
                pair, turned = (v.reshape(2, 2, 32, 128) for v in (pair, turned))
                for e in range(2):
                    first, second = (pair, turned) if e == 0 else (turned, pair)
                    tile = jnp.where(low, first[:, 0], second[:, 1])
                    qs[2 * (4 * b + u) + e] = tile.astype(jnp.bfloat16)
            for i in range(8 * b, 8 * b + 8):
                q_out(i, 0, unit_of(0, i, i)).start()
                if i % 2 == 1:
                    q_out(i, 1, unit_of(1, i, i)).start()
                else:

                    @pl.when(slot != i)
                    def _(i=i):
                        q_out(i, 1, unit_of(1, i, i)).start()

                    @pl.when(slot == i)
                    def _(i=i):
                        pltpu.make_async_copy(qs.at[i, 1], qr.at[slot], q_r).start()
        residual_out.start()
        for k in range(4):
            o_weight_out(k).start()

    pltpu.make_async_copy(qr, qr, q_r).wait()
    lane = lax.broadcasted_iota(jnp.int32, (1, 128), 1)
    key_half = jnp.where(odd == 1, 0, 1)
    key_lane = (lane // 64) == key_half
    packed = qr[...].astype(jnp.float32)
    turned = pltpu.roll(packed, 64, 2)
    first = jnp.where(odd == 1, packed, turned)
    second = jnp.where(odd == 1, turned, packed)
    placed = jnp.stack([first, second], axis=1).reshape(1024, 128)
    q2[...] = jnp.where(key_lane, placed, 0.0).astype(jnp.bfloat16)
    length = lens[s]
    one = jnp.bfloat16(1)
    column = lax.broadcasted_iota(jnp.int32, (1, SPAN), 1)
    within = (column // 128) * 256 + column % 128

    def kv_wait(c):
        pltpu.make_async_copy(kvr.at[c], kvr.at[c], kv_r.at[c]).wait()

    def score(c, rows):
        return lax.dot_general(
            q2[rows, :],
            kvr[c].reshape(SPAN, 128),
            (((1,), (1,)), ((), ())),
            preferred_element_type=jnp.float32,
        )

    def weigh(c, scores, before):
        scores = jnp.where(within + c * 128 < length, scores, MASKED)
        top = jnp.max(scores, axis=1, keepdims=True)
        top = jnp.broadcast_to(top, (ROWS, 128)) if before is None else jnp.maximum(before, top)
        probs = jnp.exp(scores - jnp.concatenate([top] * (SPAN // 128), axis=1)).astype(jnp.bfloat16)
        mixed = jnp.dot(
            probs,
            jnp.where(key_lane, one, kvr[c].reshape(SPAN, 128)),
            preferred_element_type=jnp.float32,
        )
        return top, mixed

    def block(r):
        return pl.ds(pl.multiple_of(r * ROWS, ROWS), ROWS)

    blocks = 1024 // ROWS
    kv_wait(0)
    scores = score(0, block(0))
    for r in range(blocks):
        following = score(0, block(r + 1)) if r + 1 < blocks else None
        top, mixed = weigh(0, scores, None)
        mx[block(r), :] = top
        acc[block(r), :] = mixed
        scores = following

    def c_out(k):
        return remote(cs.at[k], cr.at[s, slot], c_s, c_r, (1, seq_of(k), group))

    own_context = jnp.logical_and(decoding, odd == 0)

    kv_wait(1)
    order = [lax.rem(r + y, blocks) for r in range(blocks)]
    scores = score(1, block(order[0]))
    for n, r in enumerate(order):
        following = score(1, block(order[n + 1])) if n + 1 < blocks else None
        before = mx[block(r), :]
        top, mixed = weigh(1, scores, before)
        mixed = acc[block(r), :] * jnp.exp(before - top) + mixed
        context = mixed / pltpu.roll(mixed, 64, 1)
        context = jnp.where(key_lane, pltpu.roll(context, 64, 1), context).reshape(4, 2, 32, 128)
        cs[pl.ds(r * 4, 4)] = jnp.where(low, context[:, 0], context[:, 1]).astype(jnp.bfloat16)
        for k in range(4):
            to = r * 4 + k
            mine = jnp.logical_and(own_context, slot == to)

            @pl.when(mine)
            def _():
                pltpu.make_async_copy(cs.at[slot], cr.at[1, slot], c_r).start()

            @pl.when(jnp.logical_not(mine))
            def _(to=to):
                c_out(to).start()

        scores = following

    def x_out(c):
        return remote(cx.at[c], cx.at[c], x_s, x_r, (1, q, beside))

    def rs_out(k):
        return remote(rs.at[k], rr.at[half], rs_s, rs_r, (k // 2, q, 2 * (k % 2) + core))

    @pl.when(decoding)
    def _():
        pltpu.make_async_copy(cr, cr, c_r).wait()
        for d in range(2):
            for t in range(8):
                first = cr[d, 2 * t].astype(jnp.float32)
                second = cr[d, 2 * t + 1].astype(jnp.float32)
                at = slice(t * 128, (t + 1) * 128)
                upper = jnp.where(low, first, pltpu.roll(second, 64, 1))
                lower = jnp.where(low, pltpu.roll(first, 64, 1), second)
                cx[core, d * 64 : d * 64 + 32, at] = upper.astype(jnp.bfloat16)
                cx[core, d * 64 + 32 : d * 64 + 64, at] = lower.astype(jnp.bfloat16)
        x_out(core).start()
        pltpu.make_async_copy(wo.at[core], wo.at[core], wo_sem).wait()
        remote(wo.at[core], wo.at[1 - core], wx_s, wx_r, (1, q, beside)).wait_recv()

        def partial(c, k):
            return lax.dot_general(
                cx[c], wo[c, k], (((1,), (1,)), ((), ())), preferred_element_type=jnp.float32
            )

        far, own = 3 - half, 2 + half
        part = partial(core, far)
        x_out(1 - core).wait_recv()
        part = part + partial(1 - core, far)
        rs[far] = part.astype(jnp.bfloat16).reshape(2, 64, 512)
        rs_out(far).start()
        for k in range(2):
            part = partial(0, k) + partial(1, k)
            rs[k] = part.astype(jnp.bfloat16).reshape(2, 64, 512)
            rs_out(k).start()
        part = partial(0, own) + partial(1, own)
        rr[half] = part.astype(jnp.bfloat16).reshape(2, 64, 512)
        res[...] = xd[2 + half, :, :, pl.ds(pl.multiple_of(core * 512, 512), 512)]

    @pl.when(encoding)
    def _():
        residual_out.wait_recv()

    @pl.when(encoding)
    def _():
        pltpu.make_async_copy(rr, rr, rs_r).wait()

    @pl.when(decoding)
    def _():
        pltpu.make_async_copy(rr.at[0], rr.at[0], rs_r).wait()

    update = rr[0].astype(jnp.float32) + rr[1].astype(jnp.float32)
    out[...] = (res[...].astype(jnp.float32) + update).astype(jnp.bfloat16)

    def sent(ref, sem):
        remote(ref, ref, sem, sem, (s, q, m)).wait_send()

    @pl.when(jnp.logical_not(own_context))
    def _():
        sent(cs, c_s)

    @pl.when(own_context)
    def _():
        sent(cs.at[0:15], c_s)

    @pl.when(encoding)
    def _():
        a_dec.wait_send()
        sent(relay, fl_s)
        sent(xf.at[0], fw_s)
        for c in range(2):
            b_mem(c).wait_send()
        sent(kvs.at[0:62], kv_s)

    @pl.when(decoding)
    def _():
        sent(relay, fw_s)
        sent(xf.at[0, :, 0:160, :], fl_s)
        b_dec.wait_send()
        c_dec.wait_send()
        residual_out.wait_send()
        x_out(core).wait_send()
        sent(wo.at[core], wx_s)

        @pl.when(odd == 1)
        def _():
            sent(qs, q_s)

        @pl.when(odd == 0)
        def _():
            sent(acc.at[0:496], q_s)

        sent(rs.at[0:3], rs_s)


def on_device(memory, decoder_rows, gains, weights, lengths):
    bf16, f32 = jnp.bfloat16, jnp.float32
    anywhere = pl.BlockSpec(memory_space=pl.ANY)
    vmem = pl.BlockSpec(memory_space=pltpu.VMEM)
    dma = pltpu.SemaphoreType.DMA
    return pl.pallas_call(
        body,
        name="cross_attention",
        out_shape=jax.ShapeDtypeStruct((2, 64, 512), bf16),
        in_specs=[anywhere, anywhere, vmem, anywhere, pl.BlockSpec(memory_space=pltpu.SMEM)],
        out_specs=vmem,
        scratch_shapes=[
            pltpu.VMEM((4, 4096, 512), bf16),
            pltpu.VMEM((2, 4, 512, 1024), bf16),
            pltpu.VMEM((4, 2, 256, 1024), bf16),
            pltpu.VMEM((4, 2, 64, 1024), bf16),
            pltpu.VMEM((6, 2, PIECE, 1024), bf16),
            pltpu.VMEM((2, 256, 4096), bf16),
            pltpu.VMEM((64, 128, 128), bf16),
            pltpu.VMEM((2, 16, 128, 128), bf16),
            pltpu.VMEM((16, 2, 32, 128), bf16),
            pltpu.VMEM((16, 32, 128), bf16),
            pltpu.VMEM((1024, 128), bf16),
            pltpu.VMEM((1024, 128), f32),
            pltpu.VMEM((1024, 128), f32),
            pltpu.VMEM((16, 32, 128), bf16),
            pltpu.VMEM((2, 16, 32, 128), bf16),
            pltpu.VMEM((2, 128, 1024), bf16),
            pltpu.VMEM((4, 2, 64, 512), bf16),
            pltpu.VMEM((2, 2, 64, 512), bf16),
            pltpu.VMEM((2, 64, 512), bf16),
            dma,
            dma,
            dma,
            dma,
            dma,
            dma((16,)),
            dma((16,)),
            dma,
            dma,
            dma((2,)),
            dma((2,)),
            dma((2,)),
            dma((3,)),
            dma,
            dma((2,)),
            dma,
            dma,
            dma,
            dma,
            dma,
            dma,
            dma,
            dma,
            dma,
            dma,
        ],
        compiler_params=pltpu.CompilerParams(
            collective_id=0, has_side_effects=True, vmem_limit_bytes=60 << 20
        ),
    )(memory, decoder_rows, gains, weights, lengths)


def solution(mesh):
    in_specs = (
        P(None, "seq", "mp"),
        P(None, "seq", "mp"),
        P("segment", None),
        P("segment", None, None, "mp"),
        P(),
    )
    out_specs = P(None, "seq", ("segment", "mp"))
    return jax.shard_map(
        on_device, mesh=mesh, in_specs=in_specs, out_specs=out_specs, check_vma=False
    )
```

```python
import jax
import jax.numpy as jnp
from jax import lax
from jax.experimental import pallas as pl
from jax.experimental.pallas import tpu as pltpu
from jax.sharding import PartitionSpec as P

MESH = pl.DeviceIdType.MESH
EPS = 1e-6
MASKED = -1e30
SEQ = 16
ROWS = 256
SPAN = 2048
PIECE = 16
DIRECT = ((0, 1, 2, 3, 4), (8, 9, 10, 12, 13))
RELAYED = (5, 6, 7, 11, 14, 15)
ARRIVAL = ((0, 1), (2, 5), (3, 6), (4, 7)), ((8,), (9,), (10, 11), (12,)), ((13,), (14,), (15,), ())


def seq_of(n):
    return (n % 4) * 4 + (n // 4 + n % 4) % 4


def body(
    mem, dec, gain, w, lens, out,
    wbuf, wo, xf, xd, relay, sq, st, inv, xn, pf, po, kvs, kvr, qs, qr, q2, acc, mx, cs, cr, cx, rs, rr, res,
    w_sem, wo_sem, wx_s, wx_r, own_sem, gp_r, gf_r, fl_s, fw_s, gb_s, gb_r, st_s, st_r, d_s, d_r,
    kv_s, kv_r, q_s, q_r, c_s, c_r, x_s, x_r, rs_s, rs_r, res_s, res_r, ring_y, ring_z,
):
    s = lax.axis_index("segment")
    q = lax.axis_index("seq")
    m = lax.axis_index("mp")
    across = jnp.bitwise_xor(m, 2)
    beside = jnp.bitwise_xor(m, 1)
    corner = jnp.bitwise_xor(m, 3)
    half, core = m // 2, m % 2
    z, y = q // 4, q % 4
    slot = 4 * lax.rem(y - z + 4, 4) + z
    odd = z % 2
    group = jnp.where(s == 0, m, jnp.where(odd == 0, m, across))
    encoding = s == 0
    decoding = s == 1

    def remote(src, dst, ssem, rsem, device):
        return pltpu.make_async_remote_copy(
            src_ref=src, dst_ref=dst, send_sem=ssem, recv_sem=rsem, device_id=device, device_id_type=MESH
        )

    def kv_weight(j, t):
        return pltpu.make_async_copy(
            w.at[0, t, :, pl.ds(pl.multiple_of(j * 256, 256), 256)],
            wbuf.at[j, :, pl.ds(t * 256, 256)],
            w_sem,
        )

    def q_weight(b):
        return pltpu.make_async_copy(w.at[0, 0, :, pl.ds(b * 512, 512)], wbuf.at[b], w_sem)

    def out_rows(k, c):
        return w.at[0, 1, pl.ds(pl.multiple_of((2 * k + c) * 512, 512), 512), :]

    def o_weight(k):
        return pltpu.make_async_copy(out_rows(k, core), wo.at[core, k], wo_sem)

    def o_weight_out(k):
        return remote(out_rows(k, 1 - core), wo.at[core, k], wx_s, wx_r, (1, q, beside))

    bar = pltpu.get_barrier_semaphore()

    def hello(*device):
        pl.semaphore_signal(bar, inc=1, device_id=device, device_id_type=MESH)

    for peer in (beside, across, corner):
        hello(s, q, peer)
    hello(1 - s, q, m)
    hello(1 - s, q, across)
    ys = [4 * z + lax.rem(y + k, 4) for k in (1, 2, 3)]
    zs = [4 * lax.rem(z + k, 4) + y for k in (1, 2, 3)]
    for k in ys + zs:
        hello(s, k, m)

    own_mem = pltpu.make_async_copy(mem, xf.at[m], own_sem)

    @pl.when(encoding)
    def _():
        own_mem.start()

    @pl.when(decoding)
    def _():
        for b in range(2):
            q_weight(b).start()
        for k in range(4):
            o_weight(k).start()

    @pl.when(encoding)
    def _():
        own_mem.wait()
        for jj in range(4):
            for t in range(2):
                kv_weight(lax.rem(jj + y, 4), t).start()
        for d in range(2):

            def squares(r, _, d=d):
                rows = pl.ds(pl.multiple_of(r * 32, 32), 32)
                part = xf[m, d, rows, :].astype(jnp.float32)
                part = part * part
                total = part[:, :128]
                for k in range(1, 8):
                    total = total + part[:, k * 128 : (k + 1) * 128]
                sq[rows, :] = total
                return 0

            lax.fori_loop(0, 8, squares, 0)
            st[m, d] = jnp.broadcast_to(jnp.sum(sq[...].T, axis=0, keepdims=True), (8, 256))

    pl.semaphore_wait(bar, 11)
    for k in ys:
        pl.semaphore_signal(ring_y, inc=1, device_id=(s, k, m), device_id_type=MESH)

    def tell_z():
        pl.semaphore_wait(ring_y, 3)
        for k in zs:
            pl.semaphore_signal(ring_z, inc=1, device_id=(s, k, m), device_id_type=MESH)


    def piece(ref, p):
        return ref.at[:, pl.ds(p * PIECE, PIECE), :]

    def direct(p):
        return remote(piece(mem, p), piece(xf.at[m], p), fl_s, gp_r.at[p], (0, q, across))

    def hop(n):
        p = RELAYED[n]
        return remote(piece(mem, p), relay.at[n], fl_s, gp_r.at[p], (1, q, across))

    def relayed(n):
        p = RELAYED[n]
        return remote(relay.at[n], piece(xf.at[across], p), fw_s, gp_r.at[p], (0, q, m))

    def piece_in(p):
        return remote(piece(mem, p), piece(xf.at[across], p), fl_s, gp_r.at[p], (0, q, m))

    def forward(p):
        return remote(
            piece(xf.at[across], p), piece(xf.at[across], p), fw_s, gf_r.at[p], (0, q, beside)
        )

    def forward_in(p):
        there = jnp.bitwise_xor(beside, 2)
        return remote(piece(mem, p), piece(xf.at[there], p), fw_s, gf_r.at[p], (0, q, beside))

    b_mem = remote(mem, xf.at[m], gb_s, gb_r, (0, q, beside))

    def stats(to):
        return remote(st.at[m], st.at[m], st_s, st_r, (0, q, to))

    own_dec = pltpu.make_async_copy(dec, xd.at[m], own_sem)
    a_dec = remote(dec, xd.at[m], d_s.at[0], d_r.at[0], (1, q, across))
    b_dec = remote(dec, xd.at[m], d_s.at[0], d_r.at[1], (1, q, beside))
    c_dec = remote(xd.at[across], xd.at[across], d_s.at[1], d_r.at[2], (1, q, beside))

    low = lax.broadcasted_iota(jnp.int32, (1, 128), 1) < 64

    def tile_of(c, i, doc):
        return (c * SEQ + i) * 2 + doc

    def kv_out(at, i, doc):
        c, start, rows = at
        tile = kvs.at[tile_of(c, i, doc), pl.ds(start, rows)]
        return tile, kvr.at[c, q, pl.ds(start, rows)], kv_r.at[c]

    def unit_of(doc, i, e):
        return (0, seq_of(i), m) if doc == 0 else (1, seq_of(i), m if e % 2 == 0 else across)

    def normalise_mem(p, h):
        if p < 8:
            at, apart = p * PIECE, 128
        else:
            at, apart = 256 + (p - 8) // 4 * 128 + p % 4 * PIECE, 64
        for k in range(2):
            columns = pl.ds(pl.multiple_of((2 * h + k) * 1024, 1024), 1024)
            weight = gain[:, columns].astype(jnp.float32)
            for d in range(2):
                rows = slice(p * PIECE, (p + 1) * PIECE)
                part = xf[2 * h + k, d, rows, :].astype(jnp.float32)
                inverse = jnp.concatenate([inv[d, rows, :]] * 8, axis=1)
                xn[h, at + d * apart : at + d * apart + PIECE, k * 1024 : (k + 1) * 1024] = (
                    part * inverse * weight
                ).astype(jnp.bfloat16)

    @pl.when(encoding)
    def _():
        for to in (across, corner, beside):
            stats(to).start()
        hop(0).start()
        b_mem.start()
        hop(1).start()
        hop(2).start()
        a_dec.start()
        for n in range(3, 6):
            hop(n).start()
        pltpu.make_async_copy(st.at[0:3], st.at[0:3], st_r).wait()
        for d in range(2):
            total = (st[0, d] + st[1, d]) + (st[2, d] + st[3, d])
            inverse = lax.rsqrt(total * (1.0 / 4096) + EPS)
            inv[d] = jnp.broadcast_to(inverse[0:1, :], (128, 256)).T
        tell_z()
        b_mem.wait_recv()
        for p in range(16):
            normalise_mem(p, half)

        def ready(p):
            forward_in(p).wait_recv()
            normalise_mem(p, 1 - half)

        def pass_beside(p):
            piece_in(p).wait_recv()
            forward(p).start()

        def rows_of(h):
            return pl.ds(pl.multiple_of(h * 2048, 2048), 2048)

        pltpu.make_async_copy(wbuf, wbuf, w_sem).wait()

        for jj in range(4):
            j = lax.rem(jj + y, 4)
            pf[jj] = jnp.dot(xn[half], wbuf[j, rows_of(half), :], preferred_element_type=jnp.float32)
            for p in ARRIVAL[0][jj]:
                pass_beside(p)
        for p in sum(ARRIVAL[0], ()):
            ready(p)
        pl.semaphore_wait(ring_z, 3)

        def project(at, first, jj):
            c, start, rows = at
            j = lax.rem(jj + y, 4)
            both = pf[jj, first : first + 2 * rows, :] + jnp.dot(
                xn[1 - half, first : first + 2 * rows, :],
                wbuf[j, rows_of(1 - half), :],
                preferred_element_type=jnp.float32,
            )
            for u in range(2):
                key = pltpu.roll(both[:, u * 128 : (u + 1) * 128], 64, 1)
                value = both[:, 256 + u * 128 : 256 + (u + 1) * 128]
                for e in range(2):
                    i = 4 * j + 2 * u + e
                    tile = jnp.where(low, value, key) if e == 0 else jnp.where(low, key, value)
                    kvs[pl.ds(tile_of(c, i, 0), 2), start : start + rows] = tile.astype(
                        jnp.bfloat16
                    ).reshape(2, rows, 128)
            for e in range(4):
                i = 4 * j + e
                tile, there, sem = kv_out(at, i, 1)
                remote(tile, there, kv_s, sem, unit_of(1, i, e)).start()
                tile, there, sem = kv_out(at, i, 0)

                @pl.when(i != slot)
                def _(tile=tile, there=there, sem=sem, i=i, e=e):
                    remote(tile, there, kv_s, sem, unit_of(0, i, e)).start()

                @pl.when(i == slot)
                def _(tile=tile, there=there, sem=sem):
                    pltpu.make_async_copy(tile, there, sem).start()

        for jj in range(4):
            project((0, 0, 128), 0, jj)
            for p in ARRIVAL[1][jj]:
                pass_beside(p)
        for p in range(8, 12):
            ready(p)
        for jj in range(4):
            project((1, 0, 64), 256, jj)
            for p in ARRIVAL[2][jj]:
                pass_beside(p)
        for p in range(12, 16):
            ready(p)
        for jj in range(4):
            project((1, 64, 64), 384, jj)

    def q_out(i, doc, device):
        return remote(qs.at[i, doc], qr.at[slot], q_s, q_r, device)

    residual_out = remote(
        xd.at[m // 2, :, :, pl.ds(pl.multiple_of((m % 2) * 512, 512), 512)], res, res_s, res_r, (0, q, m)
    )

    @pl.when(decoding)
    def _():
        for p in DIRECT[0]:
            direct(p).start()
        own_dec.start()
        b_dec.start()

        def pass_on(n):
            p = RELAYED[n]
            remote(piece(mem, p), relay.at[n], fl_s, gp_r.at[p], (1, q, across)).wait_recv()
            relayed(n).start()

        pass_on(0)
        tell_z()
        pass_on(1)
        pass_on(2)
        for p in DIRECT[1]:
            direct(p).start()
        remote(dec, xd.at[across], d_s.at[0], d_r.at[0], (1, q, across)).wait_recv()
        c_dec.start()
        pass_on(3)
        pass_on(4)
        own_dec.wait()
        b_dec.wait_recv()
        c_dec.wait_recv()
        for p in range(4):
            rows = slice(p * PIECE, (p + 1) * PIECE)
            total = jnp.zeros((2, PIECE, 1), jnp.float32)
            for k in range(4):
                part = xd[k, :, rows, :].astype(jnp.float32)
                total = total + jnp.sum(part * part, axis=2, keepdims=True)
            inverse = lax.rsqrt(total * (1.0 / 4096) + EPS)
            for k in range(4):
                part = xd[k, :, rows, :].astype(jnp.float32)
                wide = part * inverse * gain[:, k * 1024 : (k + 1) * 1024].astype(jnp.float32)
                wide = wide.astype(jnp.bfloat16)
                columns = slice((k % 2) * 1024, (k % 2 + 1) * 1024)
                xn[k // 2, p * PIECE : (p + 1) * PIECE, columns] = wide[0]
                xn[k // 2, 64 + p * PIECE : 64 + (p + 1) * PIECE, columns] = wide[1]
        pass_on(5)
        pl.semaphore_wait(ring_z, 3)
        pltpu.make_async_copy(wbuf.at[0:2], wbuf.at[0:2], w_sem).wait()
        for b in range(2):
            made = jnp.dot(xn[0, :128, :], wbuf[b, :2048, :], preferred_element_type=jnp.float32)
            made = made + jnp.dot(xn[1, :128, :], wbuf[b, 2048:, :], preferred_element_type=jnp.float32)
            for u in range(4):
                pair = made[:, u * 128 : (u + 1) * 128]
                turned = pltpu.roll(pair, 64, 1)
                pair, turned = (v.reshape(2, 2, 32, 128) for v in (pair, turned))
                for e in range(2):
                    first, second = (pair, turned) if e == 0 else (turned, pair)
                    tile = jnp.where(low, first[:, 0], second[:, 1])
                    qs[2 * (4 * b + u) + e] = tile.astype(jnp.bfloat16)
            for i in range(8 * b, 8 * b + 8):
                q_out(i, 0, unit_of(0, i, i)).start()
                if i % 2 == 1:
                    q_out(i, 1, unit_of(1, i, i)).start()
                else:

                    @pl.when(slot != i)
                    def _(i=i):
                        q_out(i, 1, unit_of(1, i, i)).start()

                    @pl.when(slot == i)
                    def _(i=i):
                        pltpu.make_async_copy(qs.at[i, 1], qr.at[slot], q_r).start()
        residual_out.start()
        for k in range(4):
            o_weight_out(k).start()

    pltpu.make_async_copy(qr, qr, q_r).wait()
    lane = lax.broadcasted_iota(jnp.int32, (1, 128), 1)
    key_half = jnp.where(odd == 1, 0, 1)
    key_lane = (lane // 64) == key_half
    packed = qr[...].astype(jnp.float32)
    turned = pltpu.roll(packed, 64, 2)
    first = jnp.where(odd == 1, packed, turned)
    second = jnp.where(odd == 1, turned, packed)
    placed = jnp.stack([first, second], axis=1).reshape(1024, 128)
    q2[...] = jnp.where(key_lane, placed, 0.0).astype(jnp.bfloat16)
    length = lens[s]
    one = jnp.bfloat16(1)
    column = lax.broadcasted_iota(jnp.int32, (1, SPAN), 1)
    within = (column // 128) * 256 + column % 128

    def kv_wait(c):
        pltpu.make_async_copy(kvr.at[c], kvr.at[c], kv_r.at[c]).wait()

    def score(c, rows):
        return lax.dot_general(
            q2[rows, :],
            kvr[c].reshape(SPAN, 128),
            (((1,), (1,)), ((), ())),
            preferred_element_type=jnp.float32,
        )

    def weigh(c, scores, before):
        scores = jnp.where(within + c * 128 < length, scores, MASKED)
        top = jnp.max(scores, axis=1, keepdims=True)
        top = jnp.broadcast_to(top, (ROWS, 128)) if before is None else jnp.maximum(before, top)
        probs = jnp.exp(scores - jnp.concatenate([top] * (SPAN // 128), axis=1)).astype(jnp.bfloat16)
        mixed = jnp.dot(
            probs,
            jnp.where(key_lane, one, kvr[c].reshape(SPAN, 128)),
            preferred_element_type=jnp.float32,
        )
        return top, mixed

    def block(r):
        return pl.ds(pl.multiple_of(r * ROWS, ROWS), ROWS)

    blocks = 1024 // ROWS
    kv_wait(0)
    scores = score(0, block(0))
    for r in range(blocks):
        following = score(0, block(r + 1)) if r + 1 < blocks else None
        top, mixed = weigh(0, scores, None)
        mx[block(r), :] = top
        acc[block(r), :] = mixed
        scores = following

    def c_out(k):
        return remote(cs.at[k], cr.at[s, slot], c_s, c_r, (1, seq_of(k), group))

    own_context = jnp.logical_and(decoding, odd == 0)

    kv_wait(1)
    order = [lax.rem(r + y, blocks) for r in range(blocks)]
    scores = score(1, block(order[0]))
    for n, r in enumerate(order):
        following = score(1, block(order[n + 1])) if n + 1 < blocks else None
        before = mx[block(r), :]
        top, mixed = weigh(1, scores, before)
        mixed = acc[block(r), :] * jnp.exp(before - top) + mixed
        context = mixed / pltpu.roll(mixed, 64, 1)
        context = jnp.where(key_lane, pltpu.roll(context, 64, 1), context).reshape(4, 2, 32, 128)
        cs[pl.ds(r * 4, 4)] = jnp.where(low, context[:, 0], context[:, 1]).astype(jnp.bfloat16)
        for k in range(4):
            to = r * 4 + k
            mine = jnp.logical_and(own_context, slot == to)

            @pl.when(mine)
            def _():
                pltpu.make_async_copy(cs.at[slot], cr.at[1, slot], c_r).start()

            @pl.when(jnp.logical_not(mine))
            def _(to=to):
                c_out(to).start()

        scores = following

    def x_out(c):
        return remote(cx.at[c], cx.at[c], x_s, x_r, (1, q, beside))

    def rs_out(k):
        return remote(rs.at[k], rr.at[half], rs_s, rs_r, (k // 2, q, 2 * (k % 2) + core))

    @pl.when(decoding)
    def _():
        pltpu.make_async_copy(cr, cr, c_r).wait()
        for d in range(2):
            for t in range(8):
                first = cr[d, 2 * t].astype(jnp.float32)
                second = cr[d, 2 * t + 1].astype(jnp.float32)
                at = slice(t * 128, (t + 1) * 128)
                upper = jnp.where(low, first, pltpu.roll(second, 64, 1))
                lower = jnp.where(low, pltpu.roll(first, 64, 1), second)
                cx[core, d * 64 : d * 64 + 32, at] = upper.astype(jnp.bfloat16)
                cx[core, d * 64 + 32 : d * 64 + 64, at] = lower.astype(jnp.bfloat16)
        x_out(core).start()
        pltpu.make_async_copy(wo.at[core], wo.at[core], wo_sem).wait()
        remote(wo.at[core], wo.at[1 - core], wx_s, wx_r, (1, q, beside)).wait_recv()

        def partial(c, k):
            return lax.dot_general(
                cx[c], wo[c, k], (((1,), (1,)), ((), ())), preferred_element_type=jnp.float32
            )

        far, own = 3 - half, 2 + half
        for k in (far, 0, 1, own):
            po[k] = partial(core, k)
        x_out(1 - core).wait_recv()
        for k in (far, 0, 1):
            part = po[k] + partial(1 - core, k)
            rs[k] = part.astype(jnp.bfloat16).reshape(2, 64, 512)
            rs_out(k).start()
        part = po[own] + partial(1 - core, own)
        rr[half] = part.astype(jnp.bfloat16).reshape(2, 64, 512)
        res[...] = xd[2 + half, :, :, pl.ds(pl.multiple_of(core * 512, 512), 512)]

    @pl.when(encoding)
    def _():
        residual_out.wait_recv()

    @pl.when(encoding)
    def _():
        pltpu.make_async_copy(rr, rr, rs_r).wait()

    @pl.when(decoding)
    def _():
        pltpu.make_async_copy(rr.at[0], rr.at[0], rs_r).wait()

    update = rr[0].astype(jnp.float32) + rr[1].astype(jnp.float32)
    out[...] = (res[...].astype(jnp.float32) + update).astype(jnp.bfloat16)

    def sent(ref, sem):
        remote(ref, ref, sem, sem, (s, q, m)).wait_send()

    @pl.when(jnp.logical_not(own_context))
    def _():
        sent(cs, c_s)

    @pl.when(own_context)
    def _():
        sent(cs.at[0:15], c_s)

    @pl.when(encoding)
    def _():
        a_dec.wait_send()
        sent(relay, fl_s)
        sent(xf.at[0], fw_s)
        b_mem.wait_send()
        sent(st.at[0:3], st_s)
        sent(kvs.at[0:62], kv_s)

    @pl.when(decoding)
    def _():
        sent(relay, fw_s)
        sent(xf.at[0, :, 0:160, :], fl_s)
        b_dec.wait_send()
        c_dec.wait_send()
        residual_out.wait_send()
        x_out(core).wait_send()
        sent(wo.at[core], wx_s)

        @pl.when(odd == 1)
        def _():
            sent(qs, q_s)

        @pl.when(odd == 0)
        def _():
            sent(acc.at[0:496], q_s)

        sent(rs.at[0:3], rs_s)


def on_device(memory, decoder_rows, gains, weights, lengths):
    bf16, f32 = jnp.bfloat16, jnp.float32
    anywhere = pl.BlockSpec(memory_space=pl.ANY)
    vmem = pl.BlockSpec(memory_space=pltpu.VMEM)
    dma = pltpu.SemaphoreType.DMA
    return pl.pallas_call(
        body,
        name="cross_attention",
        out_shape=jax.ShapeDtypeStruct((2, 64, 512), bf16),
        in_specs=[anywhere, anywhere, vmem, anywhere, pl.BlockSpec(memory_space=pltpu.SMEM)],
        out_specs=vmem,
        scratch_shapes=[
            pltpu.VMEM((4, 4096, 512), bf16),
            pltpu.VMEM((2, 4, 512, 1024), bf16),
            pltpu.VMEM((4, 2, 256, 1024), bf16),
            pltpu.VMEM((4, 2, 64, 1024), bf16),
            pltpu.VMEM((6, 2, PIECE, 1024), bf16),
            pltpu.VMEM((256, 128), f32),
            pltpu.VMEM((4, 2, 8, 256), f32),
            pltpu.VMEM((2, 256, 128), f32),
            pltpu.VMEM((2, 512, 2048), bf16),
            pltpu.VMEM((4, 512, 512), f32),
            pltpu.VMEM((4, 128, 512), f32),
            pltpu.VMEM((64, 128, 128), bf16),
            pltpu.VMEM((2, 16, 128, 128), bf16),
            pltpu.VMEM((16, 2, 32, 128), bf16),
            pltpu.VMEM((16, 32, 128), bf16),
            pltpu.VMEM((1024, 128), bf16),
            pltpu.VMEM((1024, 128), f32),
            pltpu.VMEM((1024, 128), f32),
            pltpu.VMEM((16, 32, 128), bf16),
            pltpu.VMEM((2, 16, 32, 128), bf16),
            pltpu.VMEM((2, 128, 1024), bf16),
            pltpu.VMEM((4, 2, 64, 512), bf16),
            pltpu.VMEM((2, 2, 64, 512), bf16),
            pltpu.VMEM((2, 64, 512), bf16),
            dma,
            dma,
            dma,
            dma,
            dma,
            dma((16,)),
            dma((16,)),
            dma,
            dma,
            dma,
            dma,
            dma,
            dma,
            dma((2,)),
            dma((3,)),
            dma,
            dma((2,)),
            dma,
            dma,
            dma,
            dma,
            dma,
            dma,
            dma,
            dma,
            dma,
            dma,
            pltpu.SemaphoreType.REGULAR,
            pltpu.SemaphoreType.REGULAR,
        ],
        compiler_params=pltpu.CompilerParams(
            collective_id=0, has_side_effects=True, vmem_limit_bytes=60 << 20
        ),
    )(memory, decoder_rows, gains, weights, lengths)


def solution(mesh):
    in_specs = (
        P(None, "seq", "mp"),
        P(None, "seq", "mp"),
        P("segment", None),
        P("segment", None, None, "mp"),
        P(),
    )
    out_specs = P(None, "seq", ("segment", "mp"))
    return jax.shard_map(
        on_device, mesh=mesh, in_specs=in_specs, out_specs=out_specs, check_vma=False
    )
```

```python
import jax
import jax.numpy as jnp
from jax import lax
from jax.experimental import pallas as pl
from jax.experimental.pallas import tpu as pltpu
from jax.sharding import PartitionSpec as P

MESH = pl.DeviceIdType.MESH
EPS = 1e-6
MASKED = -1e30
SEQ = 16
ROWS = 256
PIECE = 16
DIRECT = (tuple(range(8)), (12, 13, 14, 15))
RELAYED = (8, 9, 10, 11)
ARRIVAL = ((0, 1), (2,), (3,), (4,)), ((), (5,), (), (6,)), ((), (8,), (9,), (10, 11)), ((12,), (13,), (14,), (15,))


def seq_of(n):
    return (n % 4) * 4 + (n // 4 + n % 4) % 4


def body(
    mem, dec, gain, w, lens, out,
    wbuf, wo, xf, xd, relay, sq, st, inv, xn, pf, po, kvs, kvr, qs, qr, q2, acc, mx, cs, cr, cx, rs, rr, res,
    w_sem, wo_sem, wx_s, wx_r, own_sem, gp_r, gf_r, fl_s, fw_s, gb_s, gb_r, st_s, st_r, d_s, d_r,
    kv_s, kv_r, q_s, q_r, c_s, c_r, x_s, x_r, rs_s, rs_r, res_s, res_r, ring_y, ring_z,
):
    s = lax.axis_index("segment")
    q = lax.axis_index("seq")
    m = lax.axis_index("mp")
    across = jnp.bitwise_xor(m, 2)
    beside = jnp.bitwise_xor(m, 1)
    corner = jnp.bitwise_xor(m, 3)
    half, core = m // 2, m % 2
    z, y = q // 4, q % 4
    slot = 4 * lax.rem(y - z + 4, 4) + z
    odd = z % 2
    group = jnp.where(s == 0, m, jnp.where(odd == 0, m, across))
    encoding = s == 0
    decoding = s == 1

    def remote(src, dst, ssem, rsem, device):
        return pltpu.make_async_remote_copy(
            src_ref=src, dst_ref=dst, send_sem=ssem, recv_sem=rsem, device_id=device, device_id_type=MESH
        )

    def kv_weight(j, t):
        return pltpu.make_async_copy(
            w.at[0, t, :, pl.ds(pl.multiple_of(j * 256, 256), 256)],
            wbuf.at[j, :, pl.ds(t * 256, 256)],
            w_sem,
        )

    def q_weight(b):
        return pltpu.make_async_copy(w.at[0, 0, :, pl.ds(b * 512, 512)], wbuf.at[b], w_sem)

    def out_rows(k, c):
        return w.at[0, 1, pl.ds(pl.multiple_of((2 * k + c) * 512, 512), 512), :]

    def o_weight(k):
        return pltpu.make_async_copy(out_rows(k, core), wo.at[core, k], wo_sem)

    def o_weight_out(k):
        return remote(out_rows(k, 1 - core), wo.at[core, k], wx_s, wx_r, (1, q, beside))

    bar = pltpu.get_barrier_semaphore()

    def hello(*device):
        pl.semaphore_signal(bar, inc=1, device_id=device, device_id_type=MESH)

    for peer in (beside, across):
        hello(s, q, peer)
    for peer in (m, across, corner):
        hello(1 - s, q, peer)
    ys = [4 * z + lax.rem(y + k, 4) for k in (1, 2, 3)]
    zs = [4 * lax.rem(z + k, 4) + y for k in (1, 2, 3)]
    for k in ys + zs:
        hello(s, k, m)

    own_mem = pltpu.make_async_copy(mem, xf.at[m], own_sem)

    own_mem.start()
    own_mem.wait()

    @pl.when(encoding)
    def _():
        for jj in range(4):
            for t in range(2):
                kv_weight(lax.rem(slot // 4 + jj, 4), t).start()

    @pl.when(decoding)
    def _():
        for b in range(2):
            q_weight(b).start()
        for k in range(4):
            o_weight(k).start()

    for d in range(2):

        def squares(r, _, d=d):
            rows = pl.ds(pl.multiple_of(r * 32, 32), 32)
            part = xf[m, d, rows, :].astype(jnp.float32)
            part = part * part
            total = part[:, :128]
            for k in range(1, 8):
                total = total + part[:, k * 128 : (k + 1) * 128]
            sq[rows, :] = total
            return 0

        lax.fori_loop(0, 8, squares, 0)
        st[m, d] = jnp.broadcast_to(jnp.sum(sq[...].T, axis=0, keepdims=True), (8, 256))

    pl.semaphore_wait(bar, 11)
    for k in ys:
        pl.semaphore_signal(ring_y, inc=1, device_id=(s, k, m), device_id_type=MESH)

    def tell_z():
        pl.semaphore_wait(ring_y, 3)
        for k in zs:
            pl.semaphore_signal(ring_z, inc=1, device_id=(s, k, m), device_id_type=MESH)


    def piece(ref, p):
        return ref.at[:, pl.ds(p * PIECE, PIECE), :]

    def direct(p):
        return remote(piece(mem, p), piece(xf.at[m], p), fl_s, gp_r.at[p], (0, q, across))

    def hop(n):
        p = RELAYED[n]
        return remote(piece(mem, p), relay.at[n], fl_s, gp_r.at[p], (1, q, across))

    def relayed(n):
        p = RELAYED[n]
        return remote(relay.at[n], piece(xf.at[across], p), fw_s, gp_r.at[p], (0, q, m))

    def piece_in(p):
        return remote(piece(mem, p), piece(xf.at[across], p), fl_s, gp_r.at[p], (0, q, m))

    def forward(p):
        return remote(
            piece(xf.at[across], p), piece(xf.at[across], p), fw_s, gf_r.at[p], (0, q, beside)
        )

    def forward_in(p):
        there = jnp.bitwise_xor(beside, 2)
        return remote(piece(mem, p), piece(xf.at[there], p), fw_s, gf_r.at[p], (0, q, beside))

    b_mem = remote(mem, xf.at[m], gb_s, gb_r, (0, q, beside))

    def stats(to):
        return remote(st.at[m], st.at[m], st_s, st_r, (0, q, to))

    own_dec = pltpu.make_async_copy(dec, xd.at[m], own_sem)
    a_dec = remote(dec, xd.at[m], d_s.at[0], d_r.at[0], (1, q, across))
    b_dec = remote(dec, xd.at[m], d_s.at[0], d_r.at[1], (1, q, beside))
    c_dec = remote(xd.at[across], xd.at[across], d_s.at[1], d_r.at[2], (1, q, beside))

    low = lax.broadcasted_iota(jnp.int32, (1, 128), 1) < 64

    def tile_of(c, i, doc):
        return (c * SEQ + i) * 2 + doc

    def kv_out(at, i, doc):
        c, start, rows = at
        tile = kvs.at[tile_of(c, i, doc), pl.ds(start, rows)]
        return tile, kvr.at[c, q, pl.ds(start, rows)], kv_r.at[c * (1 + start // 64)]

    def unit_of(doc, i, e):
        return (0, seq_of(i), m) if doc == 0 else (1, seq_of(i), jnp.where(e % 2 == 0, m, across))

    def normalise_mem(p, h):
        at = p // 4 * 128 + p % 4 * PIECE
        for k in range(2):
            columns = pl.ds(pl.multiple_of((2 * h + k) * 1024, 1024), 1024)
            weight = gain[:, columns].astype(jnp.float32)
            for d in range(2):
                rows = slice(p * PIECE, (p + 1) * PIECE)
                part = xf[2 * h + k, d, rows, :].astype(jnp.float32)
                inverse = jnp.concatenate([inv[d, rows, :]] * 8, axis=1)
                xn[h, at + d * 64 : at + d * 64 + PIECE, k * 1024 : (k + 1) * 1024] = (
                    part * inverse * weight
                ).astype(jnp.bfloat16)

    @pl.when(encoding)
    def _():
        stats(beside).start()
        a_dec.start()
        b_mem.start()
        pltpu.make_async_copy(st.at[0:3], st.at[0:3], st_r).wait()
        for d in range(2):
            total = (st[0, d] + st[1, d]) + (st[2, d] + st[3, d])
            inverse = lax.rsqrt(total * (1.0 / 4096) + EPS)
            inv[d] = jnp.broadcast_to(inverse[0:1, :], (128, 256)).T
        tell_z()
        b_mem.wait_recv()
        for p in range(16):
            normalise_mem(p, half)
        for n in range(4):
            hop(n).start()

        def ready(p):
            forward_in(p).wait_recv()
            normalise_mem(p, 1 - half)

        def pass_beside(p):
            piece_in(p).wait_recv()
            forward(p).start()

        def rows_of(h):
            return pl.ds(pl.multiple_of(h * 2048, 2048), 2048)

        pltpu.make_async_copy(wbuf, wbuf, w_sem).wait()

        for jj in range(4):
            j = lax.rem(slot // 4 + jj, 4)
            pf[jj] = jnp.dot(xn[half], wbuf[j, rows_of(half), :], preferred_element_type=jnp.float32)
            for p in ARRIVAL[0][jj]:
                pass_beside(p)
        for p in range(4):
            ready(p)
        pl.semaphore_wait(ring_z, 3)

        def project(at, first, jj):
            c, start, rows = at
            j = lax.rem(slot // 4 + jj, 4)
            both = pf[jj, first : first + 2 * rows, :] + jnp.dot(
                xn[1 - half, first : first + 2 * rows, :],
                wbuf[j, rows_of(1 - half), :],
                preferred_element_type=jnp.float32,
            )
            for u in range(2):
                key = pltpu.roll(both[:, u * 128 : (u + 1) * 128], 64, 1)
                value = both[:, 256 + u * 128 : 256 + (u + 1) * 128]
                for e in range(2):
                    i = 4 * j + 2 * u + e
                    tile = jnp.where(low, value, key) if e == 0 else jnp.where(low, key, value)
                    kvs[pl.ds(tile_of(c, i, 0), 2), start : start + rows] = tile.astype(
                        jnp.bfloat16
                    ).reshape(2, rows, 128)

            def send(e, doc):
                i = 4 * j + e
                remote(*kv_out(at, i, doc)[:2], kv_s, kv_out(at, i, doc)[2], unit_of(doc, i, e)).start()

            for k in range(4):
                e = lax.rem(z + k, 4)
                if jj + k:
                    send(e, 0)
                else:
                    pltpu.make_async_copy(*kv_out(at, slot, 0)).start()
                send(e, 1)

        for quarter in range(4):
            for jj in range(4):
                project((quarter // 2, quarter % 2 * 64, 64), quarter * 128, jj)
                if quarter < 3:
                    for p in ARRIVAL[quarter + 1][jj]:
                        pass_beside(p)
            if quarter == 0:
                ready(4)
                pass_beside(7)
                for p in range(5, 8):
                    ready(p)
            elif quarter < 3:
                for p in range(4 * quarter + 4, 4 * quarter + 8):
                    ready(p)

    def q_out(i, doc, device):
        return remote(qs.at[i, doc], qr.at[slot], q_s, q_r, device)

    residual_out = remote(
        xd.at[m // 2, :, :, pl.ds(pl.multiple_of((m % 2) * 512, 512), 512)], res, res_s, res_r, (0, q, m)
    )

    @pl.when(decoding)
    def _():
        stats(across).start()
        stats(corner).start()
        for p in DIRECT[0]:
            direct(p).start()
        own_dec.start()
        b_dec.start()

        def pass_on(n):
            p = RELAYED[n]
            remote(piece(mem, p), relay.at[n], fl_s, gp_r.at[p], (1, q, across)).wait_recv()
            relayed(n).start()

        remote(dec, xd.at[across], d_s.at[0], d_r.at[0], (1, q, across)).wait_recv()
        c_dec.start()
        tell_z()
        own_dec.wait()
        b_dec.wait_recv()
        c_dec.wait_recv()
        for p in range(4):
            rows = slice(p * PIECE, (p + 1) * PIECE)
            total = jnp.zeros((2, PIECE, 1), jnp.float32)
            for k in range(4):
                part = xd[k, :, rows, :].astype(jnp.float32)
                total = total + jnp.sum(part * part, axis=2, keepdims=True)
            inverse = lax.rsqrt(total * (1.0 / 4096) + EPS)
            for k in range(4):
                part = xd[k, :, rows, :].astype(jnp.float32)
                wide = part * inverse * gain[:, k * 1024 : (k + 1) * 1024].astype(jnp.float32)
                wide = wide.astype(jnp.bfloat16)
                columns = slice((k % 2) * 1024, (k % 2 + 1) * 1024)
                xn[k // 2, p * PIECE : (p + 1) * PIECE, columns] = wide[0]
                xn[k // 2, 64 + p * PIECE : 64 + (p + 1) * PIECE, columns] = wide[1]
        pl.semaphore_wait(ring_z, 3)
        pass_on(0)
        pass_on(1)
        pltpu.make_async_copy(wbuf.at[0:2], wbuf.at[0:2], w_sem).wait()
        for b in range(2):
            made = jnp.dot(xn[0, :128, :], wbuf[b, :2048, :], preferred_element_type=jnp.float32)
            made = made + jnp.dot(xn[1, :128, :], wbuf[b, 2048:, :], preferred_element_type=jnp.float32)
            for u in range(4):
                pair = made[:, u * 128 : (u + 1) * 128]
                turned = pltpu.roll(pair, 64, 1)
                pair, turned = (v.reshape(2, 2, 32, 128) for v in (pair, turned))
                for e in range(2):
                    first, second = (pair, turned) if e == 0 else (turned, pair)
                    tile = jnp.where(low, first[:, 0], second[:, 1])
                    qs[2 * (4 * b + u) + e] = tile.astype(jnp.bfloat16)
        pass_on(2)
        pass_on(3)
        for jj in range(4):
            for k in range(4):
                e = lax.rem(z + k, 4)
                i = 4 * lax.rem(slot // 4 + jj, 4) + e
                q_out(i, 0, unit_of(0, i, e)).start()
                if jj + k:
                    q_out(i, 1, unit_of(1, i, e)).start()
                else:

                    @pl.when(odd == 1)
                    def _(i=i, e=e):
                        q_out(i, 1, unit_of(1, i, e)).start()

                    @pl.when(odd == 0)
                    def _():
                        pltpu.make_async_copy(qs.at[slot, 1], qr.at[slot], q_r).start()

        for p in DIRECT[1]:
            direct(p).start()

    pltpu.make_async_copy(qr, qr, q_r).wait()

    @pl.when(decoding)
    def _():
        residual_out.start()
        for k in range(4):
            o_weight_out(k).start()

    lane = lax.broadcasted_iota(jnp.int32, (1, 128), 1)
    key_half = jnp.where(odd == 1, 0, 1)
    key_lane = (lane // 64) == key_half
    packed = qr[...].astype(jnp.float32)
    turned = pltpu.roll(packed, 64, 2)
    first = jnp.where(odd == 1, packed, turned)
    second = jnp.where(odd == 1, turned, packed)
    placed = jnp.stack([first, second], axis=1).reshape(1024, 128)
    q2[...] = jnp.where(key_lane, placed, 0.0).astype(jnp.bfloat16)
    length = lens[s]
    one = jnp.bfloat16(1)
    passes = ((0, 0, 128), (1, 0, 64), (1, 64, 64))

    def keys(at):
        c, start, rows = at
        return kvr[c, :, start : start + rows, :].reshape(SEQ * rows, 128)

    def kv_wait(n):
        c, start, rows = passes[n]
        part = kvr.at[c, :, pl.ds(start, rows), :]
        pltpu.make_async_copy(part, part, kv_r.at[n]).wait()

    def score(at, rows):
        return lax.dot_general(
            q2[rows, :], keys(at), (((1,), (1,)), ((), ())), preferred_element_type=jnp.float32
        )

    def weigh(at, scores, before):
        c, start, rows = at
        column = lax.broadcasted_iota(jnp.int32, (1, SEQ * rows), 1)
        position = column // rows * 256 + c * 128 + start + column % rows
        scores = jnp.where(position < length, scores, MASKED)
        top = jnp.max(scores, axis=1, keepdims=True)
        top = jnp.broadcast_to(top, (ROWS, 128)) if before is None else jnp.maximum(before, top)
        probs = jnp.exp(scores - jnp.concatenate([top] * (SEQ * rows // 128), axis=1))
        mixed = jnp.dot(
            probs.astype(jnp.bfloat16),
            jnp.where(key_lane, one, keys(at)),
            preferred_element_type=jnp.float32,
        )
        return top, mixed

    def block(r):
        return pl.ds(pl.multiple_of(r * ROWS, ROWS), ROWS)

    blocks = 1024 // ROWS
    for n in range(2):
        kv_wait(n)
        scores = score(passes[n], block(0))
        for r in range(blocks):
            following = score(passes[n], block(r + 1)) if r + 1 < blocks else None
            before = mx[block(r), :] if n else None
            top, mixed = weigh(passes[n], scores, before)
            if n:
                mixed = acc[block(r), :] * jnp.exp(before - top) + mixed
            mx[block(r), :] = top
            acc[block(r), :] = mixed
            scores = following

    def c_out(k):
        return remote(cs.at[k], cr.at[s, slot], c_s, c_r, (1, seq_of(k), group))

    own_context = jnp.logical_and(decoding, odd == 0)

    kv_wait(2)
    order = [lax.rem(slot // 4 + r, blocks) for r in range(blocks)]
    scores = score(passes[2], block(order[0]))
    for n, r in enumerate(order):
        following = score(passes[2], block(order[n + 1])) if n + 1 < blocks else None
        before = mx[block(r), :]
        top, mixed = weigh(passes[2], scores, before)
        mixed = acc[block(r), :] * jnp.exp(before - top) + mixed
        context = mixed / pltpu.roll(mixed, 64, 1)
        context = jnp.where(key_lane, pltpu.roll(context, 64, 1), context).reshape(4, 2, 32, 128)
        cs[pl.ds(r * 4, 4)] = jnp.where(low, context[:, 0], context[:, 1]).astype(jnp.bfloat16)
        for k in range(4):
            to = 4 * r + lax.rem(z + k, 4)
            if n + k:
                c_out(to).start()
            else:

                @pl.when(jnp.logical_not(own_context))
                def _(to=to):
                    c_out(to).start()

                @pl.when(own_context)
                def _():
                    pltpu.make_async_copy(cs.at[slot], cr.at[1, slot], c_r).start()

        scores = following

    def x_out(c):
        return remote(cx.at[c], cx.at[c], x_s, x_r, (1, q, beside))

    def rs_out(k):
        return remote(rs.at[k], rr.at[half], rs_s, rs_r, (k // 2, q, 2 * (k % 2) + core))

    @pl.when(decoding)
    def _():
        pltpu.make_async_copy(cr, cr, c_r).wait()
        for d in range(2):
            for t in range(8):
                first = cr[d, 2 * t].astype(jnp.float32)
                second = cr[d, 2 * t + 1].astype(jnp.float32)
                at = slice(t * 128, (t + 1) * 128)
                upper = jnp.where(low, first, pltpu.roll(second, 64, 1))
                lower = jnp.where(low, pltpu.roll(first, 64, 1), second)
                cx[core, d * 64 : d * 64 + 32, at] = upper.astype(jnp.bfloat16)
                cx[core, d * 64 + 32 : d * 64 + 64, at] = lower.astype(jnp.bfloat16)
        x_out(core).start()
        pltpu.make_async_copy(wo.at[core], wo.at[core], wo_sem).wait()
        remote(wo.at[core], wo.at[1 - core], wx_s, wx_r, (1, q, beside)).wait_recv()

        def partial(c, k):
            return lax.dot_general(
                cx[c], wo[c, k], (((1,), (1,)), ((), ())), preferred_element_type=jnp.float32
            )

        far, own = 3 - half, 2 + half
        for k in (far, 0):
            po[k] = partial(core, k)
        x_out(1 - core).wait_recv()
        for n, k in enumerate((far, 0, 1)):
            part = (po[k] if n < 2 else partial(core, k)) + partial(1 - core, k)
            rs[k] = part.astype(jnp.bfloat16).reshape(2, 64, 512)
            rs_out(k).start()
        part = partial(core, own) + partial(1 - core, own)
        rr[half] = part.astype(jnp.bfloat16).reshape(2, 64, 512)
        res[...] = xd[2 + half, :, :, pl.ds(pl.multiple_of(core * 512, 512), 512)]

    @pl.when(encoding)
    def _():
        residual_out.wait_recv()

    @pl.when(encoding)
    def _():
        pltpu.make_async_copy(rr, rr, rs_r).wait()

    @pl.when(decoding)
    def _():
        pltpu.make_async_copy(rr.at[0], rr.at[0], rs_r).wait()

    update = rr[0].astype(jnp.float32) + rr[1].astype(jnp.float32)
    out[...] = (res[...].astype(jnp.float32) + update).astype(jnp.bfloat16)

    def sent(ref, sem):
        remote(ref, ref, sem, sem, (s, q, m)).wait_send()

    @pl.when(jnp.logical_not(own_context))
    def _():
        sent(cs, c_s)

    @pl.when(own_context)
    def _():
        sent(cs.at[0:15], c_s)

    @pl.when(encoding)
    def _():
        a_dec.wait_send()
        sent(relay, fl_s)
        sent(xf.at[0], fw_s)
        b_mem.wait_send()
        sent(st.at[0], st_s)
        sent(kvs.at[0:62], kv_s)

    @pl.when(decoding)
    def _():
        sent(relay, fw_s)
        sent(st.at[0:2], st_s)
        sent(xf.at[0, :, 0:192, :], fl_s)
        b_dec.wait_send()
        c_dec.wait_send()
        residual_out.wait_send()
        x_out(core).wait_send()
        sent(wo.at[core], wx_s)

        @pl.when(odd == 1)
        def _():
            sent(qs, q_s)

        @pl.when(odd == 0)
        def _():
            sent(acc.at[0:496], q_s)

        sent(rs.at[0:3], rs_s)


def on_device(memory, decoder_rows, gains, weights, lengths):
    bf16, f32 = jnp.bfloat16, jnp.float32
    anywhere = pl.BlockSpec(memory_space=pl.ANY)
    vmem = pl.BlockSpec(memory_space=pltpu.VMEM)
    dma = pltpu.SemaphoreType.DMA
    return pl.pallas_call(
        body,
        name="cross_attention",
        out_shape=jax.ShapeDtypeStruct((2, 64, 512), bf16),
        in_specs=[anywhere, anywhere, vmem, anywhere, pl.BlockSpec(memory_space=pltpu.SMEM)],
        out_specs=vmem,
        scratch_shapes=[
            pltpu.VMEM((4, 4096, 512), bf16),
            pltpu.VMEM((2, 4, 512, 1024), bf16),
            pltpu.VMEM((4, 2, 256, 1024), bf16),
            pltpu.VMEM((4, 2, 64, 1024), bf16),
            pltpu.VMEM((4, 2, PIECE, 1024), bf16),
            pltpu.VMEM((256, 128), f32),
            pltpu.VMEM((4, 2, 8, 256), f32),
            pltpu.VMEM((2, 256, 128), f32),
            pltpu.VMEM((2, 512, 2048), bf16),
            pltpu.VMEM((4, 512, 512), f32),
            pltpu.VMEM((4, 128, 512), f32),
            pltpu.VMEM((64, 128, 128), bf16),
            pltpu.VMEM((2, 16, 128, 128), bf16),
            pltpu.VMEM((16, 2, 32, 128), bf16),
            pltpu.VMEM((16, 32, 128), bf16),
            pltpu.VMEM((1024, 128), bf16),
            pltpu.VMEM((1024, 128), f32),
            pltpu.VMEM((1024, 128), f32),
            pltpu.VMEM((16, 32, 128), bf16),
            pltpu.VMEM((2, 16, 32, 128), bf16),
            pltpu.VMEM((2, 128, 1024), bf16),
            pltpu.VMEM((4, 2, 64, 512), bf16),
            pltpu.VMEM((2, 2, 64, 512), bf16),
            pltpu.VMEM((2, 64, 512), bf16),
            dma,
            dma,
            dma,
            dma,
            dma,
            dma((16,)),
            dma((16,)),
            dma,
            dma,
            dma,
            dma,
            dma,
            dma,
            dma((2,)),
            dma((3,)),
            dma,
            dma((3,)),
            dma,
            dma,
            dma,
            dma,
            dma,
            dma,
            dma,
            dma,
            dma,
            dma,
            pltpu.SemaphoreType.REGULAR,
            pltpu.SemaphoreType.REGULAR,
        ],
        compiler_params=pltpu.CompilerParams(
            collective_id=0, has_side_effects=True, vmem_limit_bytes=60 << 20
        ),
    )(memory, decoder_rows, gains, weights, lengths)


def solution(mesh):
    in_specs = (
        P(None, "seq", "mp"),
        P(None, "seq", "mp"),
        P("segment", None),
        P("segment", None, None, "mp"),
        P(),
    )
    out_specs = P(None, "seq", ("segment", "mp"))
    return jax.shard_map(
        on_device, mesh=mesh, in_specs=in_specs, out_specs=out_specs, check_vma=False
    )
```

```python
import jax
import jax.numpy as jnp
from jax import lax
from jax.experimental import pallas as pl
from jax.experimental.pallas import tpu as pltpu
from jax.sharding import PartitionSpec as P

MESH = pl.DeviceIdType.MESH
EPS = 1e-6
MASKED = -1e30
SEQ = 16
ROWS = 256
PIECE = 16
DIRECT = (tuple(range(8)), (12, 13, 14, 15))
RELAYED = (8, 9, 10, 11)
ARRIVAL = ((0, 1), (2,), (3,), (4,)), ((), (5,), (), (6,)), ((), (8,), (9,), (10, 11)), ((12,), (13,), (14,), (15,))


def seq_of(n):
    return (n % 4) * 4 + (n // 4 + n % 4) % 4


def body(
    mem, dec, gain, w, lens, out,
    wbuf, wo, xf, xd, relay, sq, st, inv, xn, pf, po, kvs, kvr, qs, qr, q2, acc, mx, cs, cr, cx, rs, rr, res,
    w_sem, wo_sem, wx_s, wx_r, own_sem, gp_r, gf_r, fl_s, fw_s, gb_s, gb_r, st_s, st_r, d_s, d_r,
    kv_s, kv_r, q_s, q_r, c_s, c_r, x_s, x_r, rs_s, rs_r, res_s, res_r, ring_y, ring_z,
):
    s = lax.axis_index("segment")
    q = lax.axis_index("seq")
    m = lax.axis_index("mp")
    across = jnp.bitwise_xor(m, 2)
    beside = jnp.bitwise_xor(m, 1)
    corner = jnp.bitwise_xor(m, 3)
    half, core = m // 2, m % 2
    z, y = q // 4, q % 4
    slot = 4 * lax.rem(y - z + 4, 4) + z
    odd = z % 2
    group = jnp.where(s == 0, m, jnp.where(odd == 0, m, across))
    encoding = s == 0
    decoding = s == 1

    def remote(src, dst, ssem, rsem, device):
        return pltpu.make_async_remote_copy(
            src_ref=src, dst_ref=dst, send_sem=ssem, recv_sem=rsem, device_id=device, device_id_type=MESH
        )

    def kv_weight(j, t):
        return pltpu.make_async_copy(
            w.at[0, t, :, pl.ds(pl.multiple_of(j * 256, 256), 256)],
            wbuf.at[j, :, pl.ds(t * 256, 256)],
            w_sem,
        )

    def q_weight(b):
        return pltpu.make_async_copy(w.at[0, 0, :, pl.ds(b * 512, 512)], wbuf.at[b], w_sem)

    def out_rows(k, c):
        return w.at[0, 1, pl.ds(pl.multiple_of((2 * k + c) * 512, 512), 512), :]

    def o_weight(k):
        return pltpu.make_async_copy(out_rows(k, core), wo.at[core, k], wo_sem)

    def o_weight_out(k):
        return remote(out_rows(k, 1 - core), wo.at[core, k], wx_s, wx_r, (1, q, beside))

    bar = pltpu.get_barrier_semaphore()

    def hello(*device):
        pl.semaphore_signal(bar, inc=1, device_id=device, device_id_type=MESH)

    for peer in (beside, across):
        hello(s, q, peer)
    for peer in (m, across, corner):
        hello(1 - s, q, peer)
    ys = [4 * z + lax.rem(y + k, 4) for k in (1, 2, 3)]
    zs = [4 * lax.rem(z + k, 4) + y for k in (1, 2, 3)]
    for k in ys + zs:
        hello(s, k, m)

    own_mem = pltpu.make_async_copy(mem, xf.at[m], own_sem)

    own_mem.start()
    own_mem.wait()

    @pl.when(encoding)
    def _():
        for jj in range(4):
            for t in range(2):
                kv_weight(lax.rem(slot // 4 + jj, 4), t).start()

    @pl.when(decoding)
    def _():
        for b in range(2):
            q_weight(b).start()
        for k in range(4):
            o_weight(k).start()

    for d in range(2):

        def squares(r, _, d=d):
            rows = pl.ds(pl.multiple_of(r * 32, 32), 32)
            part = xf[m, d, rows, :].astype(jnp.float32)
            part = part * part
            total = part[:, :128]
            for k in range(1, 8):
                total = total + part[:, k * 128 : (k + 1) * 128]
            sq[rows, :] = total
            return 0

        lax.fori_loop(0, 8, squares, 0)
        st[m, d] = jnp.broadcast_to(jnp.sum(sq[...].T, axis=0, keepdims=True), (8, 256))

    pl.semaphore_wait(bar, 11)
    for k in ys:
        pl.semaphore_signal(ring_y, inc=1, device_id=(s, k, m), device_id_type=MESH)

    def tell_z():
        pl.semaphore_wait(ring_y, 3)
        for k in zs:
            pl.semaphore_signal(ring_z, inc=1, device_id=(s, k, m), device_id_type=MESH)


    def piece(ref, p):
        return ref.at[:, pl.ds(p * PIECE, PIECE), :]

    def direct(p):
        return remote(piece(mem, p), piece(xf.at[m], p), fl_s, gp_r.at[p], (0, q, across))

    def hop(n):
        p = RELAYED[n]
        return remote(piece(mem, p), relay.at[n], fl_s, gp_r.at[p], (1, q, across))

    def relayed(n):
        p = RELAYED[n]
        return remote(relay.at[n], piece(xf.at[across], p), fw_s, gp_r.at[p], (0, q, m))

    def piece_in(p):
        return remote(piece(mem, p), piece(xf.at[across], p), fl_s, gp_r.at[p], (0, q, m))

    def forward(p):
        return remote(
            piece(xf.at[across], p), piece(xf.at[across], p), fw_s, gf_r.at[p], (0, q, beside)
        )

    def forward_in(p):
        there = jnp.bitwise_xor(beside, 2)
        return remote(piece(mem, p), piece(xf.at[there], p), fw_s, gf_r.at[p], (0, q, beside))

    b_mem = remote(mem, xf.at[m], gb_s, gb_r, (0, q, beside))

    def stats(to):
        return remote(st.at[m], st.at[m], st_s, st_r, (0, q, to))

    own_dec = pltpu.make_async_copy(dec, xd.at[m], own_sem)
    a_dec = remote(dec, xd.at[m], d_s.at[0], d_r.at[0], (1, q, across))
    b_dec = remote(dec, xd.at[m], d_s.at[0], d_r.at[1], (1, q, beside))
    c_dec = remote(xd.at[across], xd.at[across], d_s.at[1], d_r.at[2], (1, q, beside))

    low = lax.broadcasted_iota(jnp.int32, (1, 128), 1) < 64

    def tile_of(c, i, doc):
        return (c * SEQ + i) * 2 + doc

    def kv_out(at, i, doc):
        c, start, rows = at
        tile = kvs.at[tile_of(c, i, doc), pl.ds(start, rows)]
        return tile, kvr.at[c, q, pl.ds(start, rows)], kv_r.at[c * (1 + start // 64)]

    def unit_of(doc, i, e):
        return (0, seq_of(i), m) if doc == 0 else (1, seq_of(i), jnp.where(e % 2 == 0, m, across))

    def normalise_mem(p, h):
        at = p // 4 * 128 + p % 4 * PIECE
        for k in range(2):
            columns = pl.ds(pl.multiple_of((2 * h + k) * 1024, 1024), 1024)
            weight = gain[:, columns].astype(jnp.float32)
            for d in range(2):
                rows = slice(p * PIECE, (p + 1) * PIECE)
                part = xf[2 * h + k, d, rows, :].astype(jnp.float32)
                inverse = jnp.concatenate([inv[d, rows, :]] * 8, axis=1)
                xn[h, at + d * 64 : at + d * 64 + PIECE, k * 1024 : (k + 1) * 1024] = (
                    part * inverse * weight
                ).astype(jnp.bfloat16)

    @pl.when(encoding)
    def _():
        stats(beside).start()
        a_dec.start()
        b_mem.start()
        pltpu.make_async_copy(st.at[0:3], st.at[0:3], st_r).wait()
        for d in range(2):
            total = (st[0, d] + st[1, d]) + (st[2, d] + st[3, d])
            inverse = lax.rsqrt(total * (1.0 / 4096) + EPS)
            inv[d] = jnp.broadcast_to(inverse[0:1, :], (128, 256)).T
        tell_z()
        b_mem.wait_recv()
        for p in range(16):
            normalise_mem(p, half)
        for n in range(4):
            hop(n).start()

        def ready(p):
            forward_in(p).wait_recv()
            normalise_mem(p, 1 - half)

        def pass_beside(p):
            piece_in(p).wait_recv()
            forward(p).start()

        def rows_of(h):
            return pl.ds(pl.multiple_of(h * 2048, 2048), 2048)

        pltpu.make_async_copy(wbuf, wbuf, w_sem).wait()

        for jj in range(4):
            j = lax.rem(slot // 4 + jj, 4)
            pf[jj] = jnp.dot(xn[half], wbuf[j, rows_of(half), :], preferred_element_type=jnp.float32)
            for p in ARRIVAL[0][jj]:
                pass_beside(p)
        for p in range(4):
            ready(p)
        pl.semaphore_wait(ring_z, 3)

        def project(at, first, jj):
            c, start, rows = at
            j = lax.rem(slot // 4 + jj, 4)
            both = pf[jj, first : first + 2 * rows, :] + jnp.dot(
                xn[1 - half, first : first + 2 * rows, :],
                wbuf[j, rows_of(1 - half), :],
                preferred_element_type=jnp.float32,
            )
            for u in range(2):
                key = pltpu.roll(both[:, u * 128 : (u + 1) * 128], 64, 1)
                value = both[:, 256 + u * 128 : 256 + (u + 1) * 128]
                for e in range(2):
                    i = 4 * j + 2 * u + e
                    tile = jnp.where(low, value, key) if e == 0 else jnp.where(low, key, value)
                    kvs[pl.ds(tile_of(c, i, 0), 2), start : start + rows] = tile.astype(
                        jnp.bfloat16
                    ).reshape(2, rows, 128)

            def send(e, doc):
                i = 4 * j + e
                remote(*kv_out(at, i, doc)[:2], kv_s, kv_out(at, i, doc)[2], unit_of(doc, i, e)).start()

            for k in range(4):
                e = lax.rem(z + k, 4)
                if jj + k:
                    send(e, 0)
                else:
                    pltpu.make_async_copy(*kv_out(at, slot, 0)).start()
                send(e, 1)

        for quarter in range(4):
            for jj in range(4):
                project((quarter // 2, quarter % 2 * 64, 64), quarter * 128, jj)
                if quarter < 3:
                    for p in ARRIVAL[quarter + 1][jj]:
                        pass_beside(p)
            if quarter == 0:
                ready(4)
                pass_beside(7)
                for p in range(5, 8):
                    ready(p)
            elif quarter < 3:
                for p in range(4 * quarter + 4, 4 * quarter + 8):
                    ready(p)

    def turned_rows(k):
        return pl.ds(pl.multiple_of(k * 1024, 1024), 1024)

    def turn(c):
        for k in range(4):
            wbuf[2 + c, turned_rows(k), :] = wo[c, k].T

    def q_out(i, doc, device):
        return remote(qs.at[i, doc], qr.at[slot], q_s, q_r, device)

    residual_out = remote(
        xd.at[m // 2, :, :, pl.ds(pl.multiple_of((m % 2) * 512, 512), 512)], res, res_s, res_r, (0, q, m)
    )

    @pl.when(decoding)
    def _():
        stats(across).start()
        stats(corner).start()
        for p in DIRECT[0]:
            direct(p).start()
        own_dec.start()
        b_dec.start()

        def pass_on(n):
            p = RELAYED[n]
            remote(piece(mem, p), relay.at[n], fl_s, gp_r.at[p], (1, q, across)).wait_recv()
            relayed(n).start()

        remote(dec, xd.at[across], d_s.at[0], d_r.at[0], (1, q, across)).wait_recv()
        c_dec.start()
        tell_z()
        own_dec.wait()
        b_dec.wait_recv()
        c_dec.wait_recv()
        for p in range(4):
            rows = slice(p * PIECE, (p + 1) * PIECE)
            total = jnp.zeros((2, PIECE, 1), jnp.float32)
            for k in range(4):
                part = xd[k, :, rows, :].astype(jnp.float32)
                total = total + jnp.sum(part * part, axis=2, keepdims=True)
            inverse = lax.rsqrt(total * (1.0 / 4096) + EPS)
            for k in range(4):
                part = xd[k, :, rows, :].astype(jnp.float32)
                wide = part * inverse * gain[:, k * 1024 : (k + 1) * 1024].astype(jnp.float32)
                wide = wide.astype(jnp.bfloat16)
                columns = slice((k % 2) * 1024, (k % 2 + 1) * 1024)
                xn[k // 2, p * PIECE : (p + 1) * PIECE, columns] = wide[0]
                xn[k // 2, 64 + p * PIECE : 64 + (p + 1) * PIECE, columns] = wide[1]
        pl.semaphore_wait(ring_z, 3)
        pass_on(0)
        pass_on(1)
        pltpu.make_async_copy(wbuf.at[0:2], wbuf.at[0:2], w_sem).wait()
        for b in range(2):
            made = jnp.dot(xn[0, :128, :], wbuf[b, :2048, :], preferred_element_type=jnp.float32)
            made = made + jnp.dot(xn[1, :128, :], wbuf[b, 2048:, :], preferred_element_type=jnp.float32)
            for u in range(4):
                pair = made[:, u * 128 : (u + 1) * 128]
                turned = pltpu.roll(pair, 64, 1)
                pair, turned = (v.reshape(2, 2, 32, 128) for v in (pair, turned))
                for e in range(2):
                    first, second = (pair, turned) if e == 0 else (turned, pair)
                    tile = jnp.where(low, first[:, 0], second[:, 1])
                    qs[2 * (4 * b + u) + e] = tile.astype(jnp.bfloat16)
        pass_on(2)
        pass_on(3)
        for jj in range(4):
            for k in range(4):
                e = lax.rem(z + k, 4)
                i = 4 * lax.rem(slot // 4 + jj, 4) + e
                q_out(i, 0, unit_of(0, i, e)).start()
                if jj + k:
                    q_out(i, 1, unit_of(1, i, e)).start()
                else:

                    @pl.when(odd == 1)
                    def _(i=i, e=e):
                        q_out(i, 1, unit_of(1, i, e)).start()

                    @pl.when(odd == 0)
                    def _():
                        pltpu.make_async_copy(qs.at[slot, 1], qr.at[slot], q_r).start()

        for p in DIRECT[1]:
            direct(p).start()
        pltpu.make_async_copy(wo.at[core], wo.at[core], wo_sem).wait()
        turn(core)

    pltpu.make_async_copy(qr, qr, q_r).wait()

    @pl.when(decoding)
    def _():
        residual_out.start()
        for k in range(4):
            o_weight_out(k).start()

    lane = lax.broadcasted_iota(jnp.int32, (1, 128), 1)
    key_half = jnp.where(odd == 1, 0, 1)
    key_lane = (lane // 64) == key_half
    packed = qr[...].astype(jnp.float32)
    turned = pltpu.roll(packed, 64, 2)
    first = jnp.where(odd == 1, packed, turned)
    second = jnp.where(odd == 1, turned, packed)
    placed = jnp.stack([first, second], axis=1).reshape(1024, 128)
    q2[...] = jnp.where(key_lane, placed, 0.0).astype(jnp.bfloat16)
    length = lens[s]
    one = jnp.bfloat16(1)
    passes = ((0, 0, 128), (1, 0, 64), (1, 64, 64))

    def keys(at):
        c, start, rows = at
        return kvr[c, :, start : start + rows, :].reshape(SEQ * rows, 128)

    def kv_wait(n):
        c, start, rows = passes[n]
        part = kvr.at[c, :, pl.ds(start, rows), :]
        pltpu.make_async_copy(part, part, kv_r.at[n]).wait()

    def score(at, rows):
        return lax.dot_general(
            q2[rows, :], keys(at), (((1,), (1,)), ((), ())), preferred_element_type=jnp.float32
        )

    def weigh(at, scores, before):
        c, start, rows = at
        column = lax.broadcasted_iota(jnp.int32, (1, SEQ * rows), 1)
        position = column // rows * 256 + c * 128 + start + column % rows
        scores = jnp.where(position < length, scores, MASKED)
        top = jnp.max(scores, axis=1, keepdims=True)
        top = jnp.broadcast_to(top, (ROWS, 128)) if before is None else jnp.maximum(before, top)
        probs = jnp.exp(scores - jnp.concatenate([top] * (SEQ * rows // 128), axis=1))
        mixed = jnp.dot(
            probs.astype(jnp.bfloat16),
            jnp.where(key_lane, one, keys(at)),
            preferred_element_type=jnp.float32,
        )
        return top, mixed

    def block(r):
        return pl.ds(pl.multiple_of(r * ROWS, ROWS), ROWS)

    blocks = 1024 // ROWS
    for n in range(2):
        kv_wait(n)
        scores = score(passes[n], block(0))
        for r in range(blocks):
            following = score(passes[n], block(r + 1)) if r + 1 < blocks else None
            before = mx[block(r), :] if n else None
            top, mixed = weigh(passes[n], scores, before)
            if n:
                mixed = acc[block(r), :] * jnp.exp(before - top) + mixed
            mx[block(r), :] = top
            acc[block(r), :] = mixed
            scores = following

    def c_out(k):
        return remote(cs.at[k], cr.at[s, slot], c_s, c_r, (1, seq_of(k), group))

    own_context = jnp.logical_and(decoding, odd == 0)

    kv_wait(2)
    order = [lax.rem(slot // 4 + r, blocks) for r in range(blocks)]
    scores = score(passes[2], block(order[0]))
    for n, r in enumerate(order):
        following = score(passes[2], block(order[n + 1])) if n + 1 < blocks else None
        before = mx[block(r), :]
        top, mixed = weigh(passes[2], scores, before)
        mixed = acc[block(r), :] * jnp.exp(before - top) + mixed
        context = mixed / pltpu.roll(mixed, 64, 1)
        context = jnp.where(key_lane, pltpu.roll(context, 64, 1), context).reshape(4, 2, 32, 128)
        cs[pl.ds(r * 4, 4)] = jnp.where(low, context[:, 0], context[:, 1]).astype(jnp.bfloat16)
        for k in range(4):
            to = 4 * r + lax.rem(z + k, 4)
            if n + k:
                c_out(to).start()
            else:

                @pl.when(jnp.logical_not(own_context))
                def _(to=to):
                    c_out(to).start()

                @pl.when(own_context)
                def _():
                    pltpu.make_async_copy(cs.at[slot], cr.at[1, slot], c_r).start()

        scores = following

    def x_out(c):
        return remote(cx.at[c], cx.at[c], x_s, x_r, (1, q, beside))

    def rs_out(k):
        return remote(rs.at[k], rr.at[half], rs_s, rs_r, (k // 2, q, 2 * (k % 2) + core))

    @pl.when(decoding)
    def _():
        remote(wo.at[core], wo.at[1 - core], wx_s, wx_r, (1, q, beside)).wait_recv()
        turn(1 - core)
        pltpu.make_async_copy(cr, cr, c_r).wait()
        for d in range(2):
            for t in range(8):
                first = cr[d, 2 * t].astype(jnp.float32)
                second = cr[d, 2 * t + 1].astype(jnp.float32)
                at = slice(t * 128, (t + 1) * 128)
                upper = jnp.where(low, first, pltpu.roll(second, 64, 1))
                lower = jnp.where(low, pltpu.roll(first, 64, 1), second)
                cx[core, d * 64 : d * 64 + 32, at] = upper.astype(jnp.bfloat16)
                cx[core, d * 64 + 32 : d * 64 + 64, at] = lower.astype(jnp.bfloat16)
        x_out(core).start()

        def partial(c, k):
            return jnp.dot(cx[c], wbuf[2 + c, turned_rows(k), :], preferred_element_type=jnp.float32)

        far, own = 3 - half, 2 + half
        for k in (0, far, 1, own):
            po[k] = partial(core, k)
        x_out(1 - core).wait_recv()
        for k in (0, far, 1):
            part = po[k] + partial(1 - core, k)
            rs[k] = part.astype(jnp.bfloat16).reshape(2, 64, 512)
            rs_out(k).start()
        part = po[own] + partial(1 - core, own)
        rr[half] = part.astype(jnp.bfloat16).reshape(2, 64, 512)
        res[...] = xd[2 + half, :, :, pl.ds(pl.multiple_of(core * 512, 512), 512)]

    @pl.when(encoding)
    def _():
        residual_out.wait_recv()

    @pl.when(encoding)
    def _():
        pltpu.make_async_copy(rr, rr, rs_r).wait()

    @pl.when(decoding)
    def _():
        pltpu.make_async_copy(rr.at[0], rr.at[0], rs_r).wait()

    update = rr[0].astype(jnp.float32) + rr[1].astype(jnp.float32)
    out[...] = (res[...].astype(jnp.float32) + update).astype(jnp.bfloat16)

    def sent(ref, sem):
        remote(ref, ref, sem, sem, (s, q, m)).wait_send()

    @pl.when(jnp.logical_not(own_context))
    def _():
        sent(cs, c_s)

    @pl.when(own_context)
    def _():
        sent(cs.at[0:15], c_s)

    @pl.when(encoding)
    def _():
        a_dec.wait_send()
        sent(relay, fl_s)
        sent(xf.at[0], fw_s)
        b_mem.wait_send()
        sent(st.at[0], st_s)
        sent(kvs.at[0:62], kv_s)

    @pl.when(decoding)
    def _():
        sent(relay, fw_s)
        sent(st.at[0:2], st_s)
        sent(xf.at[0, :, 0:192, :], fl_s)
        b_dec.wait_send()
        c_dec.wait_send()
        residual_out.wait_send()
        x_out(core).wait_send()
        sent(wo.at[core], wx_s)

        @pl.when(odd == 1)
        def _():
            sent(qs, q_s)

        @pl.when(odd == 0)
        def _():
            sent(acc.at[0:496], q_s)

        sent(rs.at[0:3], rs_s)


def on_device(memory, decoder_rows, gains, weights, lengths):
    bf16, f32 = jnp.bfloat16, jnp.float32
    anywhere = pl.BlockSpec(memory_space=pl.ANY)
    vmem = pl.BlockSpec(memory_space=pltpu.VMEM)
    dma = pltpu.SemaphoreType.DMA
    return pl.pallas_call(
        body,
        name="cross_attention",
        out_shape=jax.ShapeDtypeStruct((2, 64, 512), bf16),
        in_specs=[anywhere, anywhere, vmem, anywhere, pl.BlockSpec(memory_space=pltpu.SMEM)],
        out_specs=vmem,
        scratch_shapes=[
            pltpu.VMEM((4, 4096, 512), bf16),
            pltpu.VMEM((2, 4, 512, 1024), bf16),
            pltpu.VMEM((4, 2, 256, 1024), bf16),
            pltpu.VMEM((4, 2, 64, 1024), bf16),
            pltpu.VMEM((4, 2, PIECE, 1024), bf16),
            pltpu.VMEM((256, 128), f32),
            pltpu.VMEM((4, 2, 8, 256), f32),
            pltpu.VMEM((2, 256, 128), f32),
            pltpu.VMEM((2, 512, 2048), bf16),
            pltpu.VMEM((4, 512, 512), f32),
            pltpu.VMEM((4, 128, 512), f32),
            pltpu.VMEM((64, 128, 128), bf16),
            pltpu.VMEM((2, 16, 128, 128), bf16),
            pltpu.VMEM((16, 2, 32, 128), bf16),
            pltpu.VMEM((16, 32, 128), bf16),
            pltpu.VMEM((1024, 128), bf16),
            pltpu.VMEM((1024, 128), f32),
            pltpu.VMEM((1024, 128), f32),
            pltpu.VMEM((16, 32, 128), bf16),
            pltpu.VMEM((2, 16, 32, 128), bf16),
            pltpu.VMEM((2, 128, 1024), bf16),
            pltpu.VMEM((4, 2, 64, 512), bf16),
            pltpu.VMEM((2, 2, 64, 512), bf16),
            pltpu.VMEM((2, 64, 512), bf16),
            dma,
            dma,
            dma,
            dma,
            dma,
            dma((16,)),
            dma((16,)),
            dma,
            dma,
            dma,
            dma,
            dma,
            dma,
            dma((2,)),
            dma((3,)),
            dma,
            dma((3,)),
            dma,
            dma,
            dma,
            dma,
            dma,
            dma,
            dma,
            dma,
            dma,
            dma,
            pltpu.SemaphoreType.REGULAR,
            pltpu.SemaphoreType.REGULAR,
        ],
        compiler_params=pltpu.CompilerParams(
            collective_id=0, has_side_effects=True, vmem_limit_bytes=60 << 20
        ),
    )(memory, decoder_rows, gains, weights, lengths)


def solution(mesh):
    in_specs = (
        P(None, "seq", "mp"),
        P(None, "seq", "mp"),
        P("segment", None),
        P("segment", None, None, "mp"),
        P(),
    )
    out_specs = P(None, "seq", ("segment", "mp"))
    return jax.shard_map(
        on_device, mesh=mesh, in_specs=in_specs, out_specs=out_specs, check_vma=False
    )
```

```python
import jax
import jax.numpy as jnp
from jax import lax
from jax.experimental import pallas as pl
from jax.experimental.pallas import tpu as pltpu
from jax.sharding import PartitionSpec as P

MESH = pl.DeviceIdType.MESH
EPS = 1e-6
MASKED = -1e30
SEQ = 16
ROWS = 256
PIECE = 16
DIRECT = (tuple(range(8)), (12, 13, 14, 15))
RELAYED = (8, 9, 10, 11)
ARRIVAL = ((0, 1), (2,), (3,), (4,)), ((), (5,), (), (6,)), ((), (8,), (9,), (10, 11)), ((12,), (13,), (14,), (15,))


def seq_of(n):
    return (n % 4) * 4 + (n // 4 + n % 4) % 4


def body(
    mem, dec, gain, w, lens, out,
    wbuf, wo, xf, xd, relay, sq, st, inv, xn, pf, po, kvs, kvr, qs, qr, q2, acc, mx, cs, cr, cx, rs, rr, res,
    w_sem, wo_sem, wx_s, wx_r, own_sem, gp_r, gf_r, fl_s, fw_s, gb_s, gb_r, st_s, st_r, d_s, d_r,
    kv_s, kv_r, q_s, q_r, c_s, c_r, x_s, x_r, rs_s, rs_r, res_s, res_r, ring_y, ring_z,
):
    s = lax.axis_index("segment")
    q = lax.axis_index("seq")
    m = lax.axis_index("mp")
    across = jnp.bitwise_xor(m, 2)
    beside = jnp.bitwise_xor(m, 1)
    corner = jnp.bitwise_xor(m, 3)
    half, core = m // 2, m % 2
    z, y = q // 4, q % 4
    slot = 4 * lax.rem(y - z + 4, 4) + z
    odd = z % 2
    group = jnp.where(s == 0, m, jnp.where(odd == 0, m, across))
    encoding = s == 0
    decoding = s == 1

    def remote(src, dst, ssem, rsem, device):
        return pltpu.make_async_remote_copy(
            src_ref=src, dst_ref=dst, send_sem=ssem, recv_sem=rsem, device_id=device, device_id_type=MESH
        )

    def kv_weight(j, t):
        return pltpu.make_async_copy(
            w.at[0, t, :, pl.ds(pl.multiple_of(j * 256, 256), 256)],
            wbuf.at[j, :, pl.ds(t * 256, 256)],
            w_sem,
        )

    def q_weight(b):
        return pltpu.make_async_copy(w.at[0, 0, :, pl.ds(b * 512, 512)], wbuf.at[b], w_sem)

    def out_rows(k, c):
        return w.at[0, 1, pl.ds(pl.multiple_of((2 * k + c) * 512, 512), 512), :]

    def o_weight(k):
        return pltpu.make_async_copy(out_rows(k, core), wo.at[core, k], wo_sem)

    def o_weight_out(k):
        return remote(out_rows(k, 1 - core), wo.at[core, k], wx_s, wx_r, (1, q, beside))

    bar = pltpu.get_barrier_semaphore()

    def hello(*device):
        pl.semaphore_signal(bar, inc=1, device_id=device, device_id_type=MESH)

    for peer in (beside, across):
        hello(s, q, peer)
    for peer in (m, across, corner):
        hello(1 - s, q, peer)
    ys = [4 * z + lax.rem(y + k, 4) for k in (1, 2, 3)]
    zs = [4 * lax.rem(z + k, 4) + y for k in (1, 2, 3)]
    for k in ys + zs:
        hello(s, k, m)

    own_mem = pltpu.make_async_copy(mem, xf.at[m], own_sem)

    own_mem.start()
    own_mem.wait()

    @pl.when(encoding)
    def _():
        for jj in range(4):
            for t in range(2):
                kv_weight(lax.rem(slot // 4 + jj, 4), t).start()

    @pl.when(decoding)
    def _():
        for b in range(2):
            q_weight(b).start()
        for k in range(4):
            o_weight(k).start()

    for d in range(2):

        def squares(r, _, d=d):
            rows = pl.ds(pl.multiple_of(r * 32, 32), 32)
            part = xf[m, d, rows, :].astype(jnp.float32)
            part = part * part
            total = part[:, :128]
            for k in range(1, 8):
                total = total + part[:, k * 128 : (k + 1) * 128]
            sq[rows, :] = total
            return 0

        lax.fori_loop(0, 8, squares, 0)
        st[m, d] = jnp.broadcast_to(jnp.sum(sq[...].T, axis=0, keepdims=True), (8, 256))

    pl.semaphore_wait(bar, 11)
    for k in ys:
        pl.semaphore_signal(ring_y, inc=1, device_id=(s, k, m), device_id_type=MESH)

    def tell_z():
        pl.semaphore_wait(ring_y, 3)
        for k in zs:
            pl.semaphore_signal(ring_z, inc=1, device_id=(s, k, m), device_id_type=MESH)


    def piece(ref, p):
        return ref.at[:, pl.ds(p * PIECE, PIECE), :]

    def direct(p):
        return remote(piece(mem, p), piece(xf.at[m], p), fl_s, gp_r.at[p], (0, q, across))

    def hop(n):
        p = RELAYED[n]
        return remote(piece(mem, p), relay.at[n], fl_s, gp_r.at[p], (1, q, across))

    def relayed(n):
        p = RELAYED[n]
        return remote(relay.at[n], piece(xf.at[across], p), fw_s, gp_r.at[p], (0, q, m))

    def piece_in(p):
        return remote(piece(mem, p), piece(xf.at[across], p), fl_s, gp_r.at[p], (0, q, m))

    def forward(p):
        return remote(
            piece(xf.at[across], p), piece(xf.at[across], p), fw_s, gf_r.at[p], (0, q, beside)
        )

    def forward_in(p):
        there = jnp.bitwise_xor(beside, 2)
        return remote(piece(mem, p), piece(xf.at[there], p), fw_s, gf_r.at[p], (0, q, beside))

    b_mem = remote(mem, xf.at[m], gb_s, gb_r, (0, q, beside))

    def stats(to):
        return remote(st.at[m], st.at[m], st_s, st_r, (0, q, to))

    own_dec = pltpu.make_async_copy(dec, xd.at[m], own_sem)
    a_dec = remote(dec, xd.at[m], d_s.at[0], d_r.at[0], (1, q, across))
    b_dec = remote(dec, xd.at[m], d_s.at[0], d_r.at[1], (1, q, beside))
    c_dec = remote(xd.at[across], xd.at[across], d_s.at[1], d_r.at[2], (1, q, beside))

    low = lax.broadcasted_iota(jnp.int32, (1, 128), 1) < 64

    def tile_of(c, i, doc):
        return (c * SEQ + i) * 2 + doc

    def kv_out(at, i, doc):
        c, start, rows = at
        tile = kvs.at[tile_of(c, i, doc), pl.ds(start, rows)]
        return tile, kvr.at[c, q, pl.ds(start, rows)], kv_r.at[c * (1 + start // 64)]

    def unit_of(doc, i, e):
        return (0, seq_of(i), m) if doc == 0 else (1, seq_of(i), jnp.where(e % 2 == 0, m, across))

    def normalise_mem(p, h):
        at = p // 4 * 128 + p % 4 * PIECE
        for k in range(2):
            columns = pl.ds(pl.multiple_of((2 * h + k) * 1024, 1024), 1024)
            weight = gain[:, columns].astype(jnp.float32)
            for d in range(2):
                rows = slice(p * PIECE, (p + 1) * PIECE)
                part = xf[2 * h + k, d, rows, :].astype(jnp.float32)
                inverse = jnp.concatenate([inv[d, rows, :]] * 8, axis=1)
                xn[h, at + d * 64 : at + d * 64 + PIECE, k * 1024 : (k + 1) * 1024] = (
                    part * inverse * weight
                ).astype(jnp.bfloat16)

    @pl.when(encoding)
    def _():
        stats(beside).start()
        a_dec.start()
        b_mem.start()
        pltpu.make_async_copy(st.at[0:3], st.at[0:3], st_r).wait()
        for d in range(2):
            total = (st[0, d] + st[1, d]) + (st[2, d] + st[3, d])
            inverse = lax.rsqrt(total * (1.0 / 4096) + EPS)
            inv[d] = jnp.broadcast_to(inverse[0:1, :], (128, 256)).T
        tell_z()
        b_mem.wait_recv()
        for p in range(16):
            normalise_mem(p, half)
        for n in range(4):
            hop(n).start()

        def ready(p):
            forward_in(p).wait_recv()
            normalise_mem(p, 1 - half)

        def pass_beside(p):
            piece_in(p).wait_recv()
            forward(p).start()

        def rows_of(h):
            return pl.ds(pl.multiple_of(h * 2048, 2048), 2048)

        pltpu.make_async_copy(wbuf, wbuf, w_sem).wait()

        for jj in range(4):
            j = lax.rem(slot // 4 + jj, 4)
            pf[jj] = jnp.dot(xn[half], wbuf[j, rows_of(half), :], preferred_element_type=jnp.float32)
            for p in ARRIVAL[0][jj]:
                pass_beside(p)
        for p in range(4):
            ready(p)
        pl.semaphore_wait(ring_z, 3)

        def project(at, first, jj):
            c, start, rows = at
            j = lax.rem(slot // 4 + jj, 4)
            both = pf[jj, first : first + 2 * rows, :] + jnp.dot(
                xn[1 - half, first : first + 2 * rows, :],
                wbuf[j, rows_of(1 - half), :],
                preferred_element_type=jnp.float32,
            )
            for u in range(2):
                key = pltpu.roll(both[:, u * 128 : (u + 1) * 128], 64, 1)
                value = both[:, 256 + u * 128 : 256 + (u + 1) * 128]
                for e in range(2):
                    i = 4 * j + 2 * u + e
                    tile = jnp.where(low, value, key) if e == 0 else jnp.where(low, key, value)
                    kvs[pl.ds(tile_of(c, i, 0), 2), start : start + rows] = tile.astype(
                        jnp.bfloat16
                    ).reshape(2, rows, 128)

            def send(e, doc):
                i = 4 * j + e
                remote(*kv_out(at, i, doc)[:2], kv_s, kv_out(at, i, doc)[2], unit_of(doc, i, e)).start()

            for k in range(4):
                e = lax.rem(z + k, 4)
                if jj + k:
                    send(e, 0)
                else:
                    pltpu.make_async_copy(*kv_out(at, slot, 0)).start()
                send(e, 1)

        for quarter in range(4):
            for jj in range(4):
                project((quarter // 2, quarter % 2 * 64, 64), quarter * 128, jj)
                if quarter < 3:
                    for p in ARRIVAL[quarter + 1][jj]:
                        pass_beside(p)
            if quarter == 0:
                ready(4)
                pass_beside(7)
                for p in range(5, 8):
                    ready(p)
            elif quarter < 3:
                for p in range(4 * quarter + 4, 4 * quarter + 8):
                    ready(p)

    def turned_rows(k):
        return pl.ds(pl.multiple_of(k * 1024, 1024), 1024)

    def turn(c):
        for k in range(4):
            wbuf[2 + c, turned_rows(k), :] = wo[c, k].T

    def q_out(i, doc, device):
        return remote(qs.at[i, doc], qr.at[slot], q_s, q_r, device)

    residual_out = remote(
        xd.at[m // 2, :, :, pl.ds(pl.multiple_of((m % 2) * 512, 512), 512)], res, res_s, res_r, (0, q, m)
    )

    @pl.when(decoding)
    def _():
        stats(across).start()
        stats(corner).start()
        for p in DIRECT[0]:
            direct(p).start()
        own_dec.start()
        b_dec.start()

        def pass_on(n):
            p = RELAYED[n]
            remote(piece(mem, p), relay.at[n], fl_s, gp_r.at[p], (1, q, across)).wait_recv()
            relayed(n).start()

        remote(dec, xd.at[across], d_s.at[0], d_r.at[0], (1, q, across)).wait_recv()
        c_dec.start()
        tell_z()
        own_dec.wait()
        b_dec.wait_recv()
        c_dec.wait_recv()
        for p in range(4):
            rows = slice(p * PIECE, (p + 1) * PIECE)
            total = jnp.zeros((2, PIECE, 1), jnp.float32)
            for k in range(4):
                part = xd[k, :, rows, :].astype(jnp.float32)
                total = total + jnp.sum(part * part, axis=2, keepdims=True)
            inverse = lax.rsqrt(total * (1.0 / 4096) + EPS)
            for k in range(4):
                part = xd[k, :, rows, :].astype(jnp.float32)
                wide = part * inverse * gain[:, k * 1024 : (k + 1) * 1024].astype(jnp.float32)
                wide = wide.astype(jnp.bfloat16)
                columns = slice((k % 2) * 1024, (k % 2 + 1) * 1024)
                xn[k // 2, p * PIECE : (p + 1) * PIECE, columns] = wide[0]
                xn[k // 2, 64 + p * PIECE : 64 + (p + 1) * PIECE, columns] = wide[1]
        pl.semaphore_wait(ring_z, 3)
        pass_on(0)
        pass_on(1)
        pltpu.make_async_copy(wbuf.at[0:2], wbuf.at[0:2], w_sem).wait()
        for b in range(2):
            made = jnp.dot(xn[0, :128, :], wbuf[b, :2048, :], preferred_element_type=jnp.float32)
            made = made + jnp.dot(xn[1, :128, :], wbuf[b, 2048:, :], preferred_element_type=jnp.float32)
            for u in range(4):
                pair = made[:, u * 128 : (u + 1) * 128]
                turned = pltpu.roll(pair, 64, 1)
                pair, turned = (v.reshape(2, 2, 32, 128) for v in (pair, turned))
                for e in range(2):
                    first, second = (pair, turned) if e == 0 else (turned, pair)
                    tile = jnp.where(low, first[:, 0], second[:, 1])
                    qs[2 * (4 * b + u) + e] = tile.astype(jnp.bfloat16)
        pass_on(2)
        pass_on(3)
        for jj in range(4):
            for k in range(4):
                e = lax.rem(z + k, 4)
                i = 4 * lax.rem(slot // 4 + jj, 4) + e
                q_out(i, 0, unit_of(0, i, e)).start()
                if jj + k:
                    q_out(i, 1, unit_of(1, i, e)).start()
                else:

                    @pl.when(odd == 1)
                    def _(i=i, e=e):
                        q_out(i, 1, unit_of(1, i, e)).start()

                    @pl.when(odd == 0)
                    def _():
                        pltpu.make_async_copy(qs.at[slot, 1], qr.at[slot], q_r).start()

        for p in DIRECT[1]:
            direct(p).start()
        pltpu.make_async_copy(wo.at[core], wo.at[core], wo_sem).wait()
        turn(core)

    pltpu.make_async_copy(qr, qr, q_r).wait()

    @pl.when(decoding)
    def _():
        residual_out.start()
        for k in range(4):
            o_weight_out(k).start()

    lane = lax.broadcasted_iota(jnp.int32, (1, 128), 1)
    key_half = jnp.where(odd == 1, 0, 1)
    key_lane = (lane // 64) == key_half
    packed = qr[...].astype(jnp.float32)
    turned = pltpu.roll(packed, 64, 2)
    first = jnp.where(odd == 1, packed, turned)
    second = jnp.where(odd == 1, turned, packed)
    placed = jnp.stack([first, second], axis=1).reshape(1024, 128)
    q2[...] = jnp.where(key_lane, placed, 0.0).astype(jnp.bfloat16)
    length = lens[s]
    one = jnp.bfloat16(1)
    passes = ((0, 0, 128), (1, 0, 64), (1, 64, 64))

    def keys(at):
        c, start, rows = at
        return kvr[c, :, start : start + rows, :].reshape(SEQ * rows, 128)

    def kv_wait(n):
        c, start, rows = passes[n]
        part = kvr.at[c, :, pl.ds(start, rows), :]
        pltpu.make_async_copy(part, part, kv_r.at[n]).wait()

    def score(at, rows):
        return lax.dot_general(
            q2[rows, :], keys(at), (((1,), (1,)), ((), ())), preferred_element_type=jnp.float32
        )

    def weigh(at, scores, before):
        c, start, rows = at
        column = lax.broadcasted_iota(jnp.int32, (1, SEQ * rows), 1)
        position = column // rows * 256 + c * 128 + start + column % rows
        scores = jnp.where(position < length, scores, MASKED)
        top = jnp.max(scores, axis=1, keepdims=True)
        top = jnp.broadcast_to(top, (ROWS, 128)) if before is None else jnp.maximum(before, top)
        probs = jnp.exp(scores - jnp.concatenate([top] * (SEQ * rows // 128), axis=1))
        mixed = jnp.dot(
            probs.astype(jnp.bfloat16),
            jnp.where(key_lane, one, keys(at)),
            preferred_element_type=jnp.float32,
        )
        return top, mixed

    def block(r):
        return pl.ds(pl.multiple_of(r * ROWS, ROWS), ROWS)

    blocks = 1024 // ROWS
    for n in range(2):
        kv_wait(n)
        scores = score(passes[n], block(0))
        for r in range(blocks):
            following = score(passes[n], block(r + 1)) if r + 1 < blocks else None
            before = mx[block(r), :] if n else None
            top, mixed = weigh(passes[n], scores, before)
            if n:
                mixed = acc[block(r), :] * jnp.exp(before - top) + mixed
            mx[block(r), :] = top
            acc[block(r), :] = mixed
            scores = following

    def c_out(k):
        return remote(cs.at[k], cr.at[s, slot], c_s, c_r, (1, seq_of(k), group))

    own_context = jnp.logical_and(decoding, odd == 0)

    kv_wait(2)
    order = [lax.rem(slot // 4 + r, blocks) for r in range(blocks)]

    def finish(n, mixed):
        r = order[n]
        context = mixed / pltpu.roll(mixed, 64, 1)
        context = jnp.where(key_lane, pltpu.roll(context, 64, 1), context).reshape(4, 2, 32, 128)
        cs[pl.ds(r * 4, 4)] = jnp.where(low, context[:, 0], context[:, 1]).astype(jnp.bfloat16)
        for k in range(4):
            to = 4 * r + lax.rem(z + k, 4)
            if n + k:
                c_out(to).start()
            else:

                @pl.when(jnp.logical_not(own_context))
                def _(to=to):
                    c_out(to).start()

                @pl.when(own_context)
                def _():
                    pltpu.make_async_copy(cs.at[slot], cr.at[1, slot], c_r).start()

    scores = score(passes[2], block(order[0]))
    mixed = None
    for n, r in enumerate(order):
        following = score(passes[2], block(order[n + 1])) if n + 1 < blocks else None
        before = mx[block(r), :]
        top, added = weigh(passes[2], scores, before)
        added = acc[block(r), :] * jnp.exp(before - top) + added
        if n:
            finish(n - 1, mixed)
        mixed, scores = added, following
    finish(blocks - 1, mixed)

    def x_out(c):
        return remote(cx.at[c], cx.at[c], x_s, x_r, (1, q, beside))

    def rs_out(k):
        return remote(rs.at[k], rr.at[half], rs_s, rs_r, (k // 2, q, 2 * (k % 2) + core))

    @pl.when(decoding)
    def _():
        remote(wo.at[core], wo.at[1 - core], wx_s, wx_r, (1, q, beside)).wait_recv()
        turn(1 - core)
        pltpu.make_async_copy(cr, cr, c_r).wait()
        for d in range(2):
            for t in range(8):
                first = cr[d, 2 * t].astype(jnp.float32)
                second = cr[d, 2 * t + 1].astype(jnp.float32)
                at = slice(t * 128, (t + 1) * 128)
                upper = jnp.where(low, first, pltpu.roll(second, 64, 1))
                lower = jnp.where(low, pltpu.roll(first, 64, 1), second)
                cx[core, d * 64 : d * 64 + 32, at] = upper.astype(jnp.bfloat16)
                cx[core, d * 64 + 32 : d * 64 + 64, at] = lower.astype(jnp.bfloat16)
        x_out(core).start()

        def partial(c, k):
            return jnp.dot(cx[c], wbuf[2 + c, turned_rows(k), :], preferred_element_type=jnp.float32)

        far, own = 3 - half, 2 + half
        for k in (0, far, 1, own):
            po[k] = partial(core, k)
        x_out(1 - core).wait_recv()
        for k in (0, far, 1):
            part = po[k] + partial(1 - core, k)
            rs[k] = part.astype(jnp.bfloat16).reshape(2, 64, 512)
            rs_out(k).start()
        part = po[own] + partial(1 - core, own)
        rr[half] = part.astype(jnp.bfloat16).reshape(2, 64, 512)
        res[...] = xd[2 + half, :, :, pl.ds(pl.multiple_of(core * 512, 512), 512)]

    @pl.when(encoding)
    def _():
        residual_out.wait_recv()

    @pl.when(encoding)
    def _():
        pltpu.make_async_copy(rr, rr, rs_r).wait()

    @pl.when(decoding)
    def _():
        pltpu.make_async_copy(rr.at[0], rr.at[0], rs_r).wait()

    update = rr[0].astype(jnp.float32) + rr[1].astype(jnp.float32)
    out[...] = (res[...].astype(jnp.float32) + update).astype(jnp.bfloat16)

    def sent(ref, sem):
        remote(ref, ref, sem, sem, (s, q, m)).wait_send()

    @pl.when(jnp.logical_not(own_context))
    def _():
        sent(cs, c_s)

    @pl.when(own_context)
    def _():
        sent(cs.at[0:15], c_s)

    @pl.when(encoding)
    def _():
        a_dec.wait_send()
        sent(relay, fl_s)
        sent(xf.at[0], fw_s)
        b_mem.wait_send()
        sent(st.at[0], st_s)
        sent(kvs.at[0:62], kv_s)

    @pl.when(decoding)
    def _():
        sent(relay, fw_s)
        sent(st.at[0:2], st_s)
        sent(xf.at[0, :, 0:192, :], fl_s)
        b_dec.wait_send()
        c_dec.wait_send()
        residual_out.wait_send()
        x_out(core).wait_send()
        sent(wo.at[core], wx_s)

        @pl.when(odd == 1)
        def _():
            sent(qs, q_s)

        @pl.when(odd == 0)
        def _():
            sent(acc.at[0:496], q_s)

        sent(rs.at[0:3], rs_s)


def on_device(memory, decoder_rows, gains, weights, lengths):
    bf16, f32 = jnp.bfloat16, jnp.float32
    anywhere = pl.BlockSpec(memory_space=pl.ANY)
    vmem = pl.BlockSpec(memory_space=pltpu.VMEM)
    dma = pltpu.SemaphoreType.DMA
    return pl.pallas_call(
        body,
        name="cross_attention",
        out_shape=jax.ShapeDtypeStruct((2, 64, 512), bf16),
        in_specs=[anywhere, anywhere, vmem, anywhere, pl.BlockSpec(memory_space=pltpu.SMEM)],
        out_specs=vmem,
        scratch_shapes=[
            pltpu.VMEM((4, 4096, 512), bf16),
            pltpu.VMEM((2, 4, 512, 1024), bf16),
            pltpu.VMEM((4, 2, 256, 1024), bf16),
            pltpu.VMEM((4, 2, 64, 1024), bf16),
            pltpu.VMEM((4, 2, PIECE, 1024), bf16),
            pltpu.VMEM((256, 128), f32),
            pltpu.VMEM((4, 2, 8, 256), f32),
            pltpu.VMEM((2, 256, 128), f32),
            pltpu.VMEM((2, 512, 2048), bf16),
            pltpu.VMEM((4, 512, 512), f32),
            pltpu.VMEM((4, 128, 512), f32),
            pltpu.VMEM((64, 128, 128), bf16),
            pltpu.VMEM((2, 16, 128, 128), bf16),
            pltpu.VMEM((16, 2, 32, 128), bf16),
            pltpu.VMEM((16, 32, 128), bf16),
            pltpu.VMEM((1024, 128), bf16),
            pltpu.VMEM((1024, 128), f32),
            pltpu.VMEM((1024, 128), f32),
            pltpu.VMEM((16, 32, 128), bf16),
            pltpu.VMEM((2, 16, 32, 128), bf16),
            pltpu.VMEM((2, 128, 1024), bf16),
            pltpu.VMEM((4, 2, 64, 512), bf16),
            pltpu.VMEM((2, 2, 64, 512), bf16),
            pltpu.VMEM((2, 64, 512), bf16),
            dma,
            dma,
            dma,
            dma,
            dma,
            dma((16,)),
            dma((16,)),
            dma,
            dma,
            dma,
            dma,
            dma,
            dma,
            dma((2,)),
            dma((3,)),
            dma,
            dma((3,)),
            dma,
            dma,
            dma,
            dma,
            dma,
            dma,
            dma,
            dma,
            dma,
            dma,
            pltpu.SemaphoreType.REGULAR,
            pltpu.SemaphoreType.REGULAR,
        ],
        compiler_params=pltpu.CompilerParams(
            collective_id=0, has_side_effects=True, vmem_limit_bytes=60 << 20
        ),
    )(memory, decoder_rows, gains, weights, lengths)


def solution(mesh):
    in_specs = (
        P(None, "seq", "mp"),
        P(None, "seq", "mp"),
        P("segment", None),
        P("segment", None, None, "mp"),
        P(),
    )
    out_specs = P(None, "seq", ("segment", "mp"))
    return jax.shard_map(
        on_device, mesh=mesh, in_specs=in_specs, out_specs=out_specs, check_vma=False
    )
```

```python
import jax
import jax.numpy as jnp
from jax import lax
from jax.experimental import pallas as pl
from jax.experimental.pallas import tpu as pltpu
from jax.sharding import PartitionSpec as P

MESH = pl.DeviceIdType.MESH
EPS = 1e-6
MASKED = -1e30
SEQ = 16
ROWS = 256
PIECE = 16
DIRECT = (tuple(range(8)), (12, 13, 14, 15))
RELAYED = (8, 9, 10, 11)
ARRIVAL = ((0, 1), (2,), (3,), (4,)), ((), (5,), (), (6,)), ((), (8,), (9,), (10, 11)), ((12,), (13,), (14,), (15,))


def seq_of(n):
    return (n % 4) * 4 + (n // 4 + n % 4) % 4


def body(
    mem, dec, gain, w, lens, out,
    wbuf, wo, xf, xd, relay, sq, st, inv, xn, pf, po, kvs, kvr, qs, qr, q2, acc, mx, cs, cr, cx, rs, rr, res,
    w_sem, wo_sem, wx_s, wx_r, own_sem, gp_r, gf_r, fl_s, fw_s, gb_s, gb_r, st_s, st_r, d_s, d_r,
    kv_s, kv_r, q_s, q_r, c_s, c_r, x_s, x_r, rs_s, rs_r, res_s, res_r, ring_y, ring_z,
):
    s = lax.axis_index("segment")
    q = lax.axis_index("seq")
    m = lax.axis_index("mp")
    across = jnp.bitwise_xor(m, 2)
    beside = jnp.bitwise_xor(m, 1)
    corner = jnp.bitwise_xor(m, 3)
    half, core = m // 2, m % 2
    z, y = q // 4, q % 4
    slot = 4 * lax.rem(y - z + 4, 4) + z
    odd = z % 2
    group = jnp.where(s == 0, m, jnp.where(odd == 0, m, across))
    encoding = s == 0
    decoding = s == 1

    def remote(src, dst, ssem, rsem, device):
        return pltpu.make_async_remote_copy(
            src_ref=src, dst_ref=dst, send_sem=ssem, recv_sem=rsem, device_id=device, device_id_type=MESH
        )

    def kv_weight(j, t):
        return pltpu.make_async_copy(
            w.at[0, t, :, pl.ds(pl.multiple_of(j * 256, 256), 256)],
            wbuf.at[j, :, pl.ds(t * 256, 256)],
            w_sem,
        )

    def q_weight(b):
        return pltpu.make_async_copy(w.at[0, 0, :, pl.ds(b * 512, 512)], wbuf.at[b], w_sem)

    def out_rows(k, c):
        return w.at[0, 1, pl.ds(pl.multiple_of((2 * k + c) * 512, 512), 512), :]

    def o_weight(k):
        return pltpu.make_async_copy(out_rows(k, core), wo.at[core, k], wo_sem)

    def o_weight_out(k):
        return remote(out_rows(k, 1 - core), wo.at[core, k], wx_s, wx_r, (1, q, beside))

    bar = pltpu.get_barrier_semaphore()

    def hello(*device):
        pl.semaphore_signal(bar, inc=1, device_id=device, device_id_type=MESH)

    for peer in (beside, across):
        hello(s, q, peer)
    for peer in (m, across, corner):
        hello(1 - s, q, peer)
    ys = [4 * z + lax.rem(y + k, 4) for k in (1, 2, 3)]
    zs = [4 * lax.rem(z + k, 4) + y for k in (1, 2, 3)]
    for k in ys + zs:
        hello(s, k, m)

    own_mem = pltpu.make_async_copy(mem, xf.at[m], own_sem)

    own_mem.start()
    own_mem.wait()

    @pl.when(encoding)
    def _():
        for jj in range(4):
            for t in range(2):
                kv_weight(lax.rem(slot // 4 + jj, 4), t).start()

    @pl.when(decoding)
    def _():
        for b in range(2):
            q_weight(b).start()
        for k in range(4):
            o_weight(k).start()

    for d in range(2):

        def squares(r, _, d=d):
            rows = pl.ds(pl.multiple_of(r * 32, 32), 32)
            part = xf[m, d, rows, :].astype(jnp.float32)
            part = part * part
            total = part[:, :128]
            for k in range(1, 8):
                total = total + part[:, k * 128 : (k + 1) * 128]
            sq[rows, :] = total
            return 0

        lax.fori_loop(0, 8, squares, 0)
        st[m, d] = jnp.broadcast_to(jnp.sum(sq[...].T, axis=0, keepdims=True), (8, 256))

    pl.semaphore_wait(bar, 11)
    for k in ys:
        pl.semaphore_signal(ring_y, inc=1, device_id=(s, k, m), device_id_type=MESH)

    def tell_z():
        pl.semaphore_wait(ring_y, 3)
        for k in zs:
            pl.semaphore_signal(ring_z, inc=1, device_id=(s, k, m), device_id_type=MESH)


    def piece(ref, p):
        return ref.at[:, pl.ds(p * PIECE, PIECE), :]

    def direct(p):
        return remote(piece(mem, p), piece(xf.at[m], p), fl_s, gp_r.at[p], (0, q, across))

    def hop(n):
        p = RELAYED[n]
        return remote(piece(mem, p), relay.at[n], fl_s, gp_r.at[p], (1, q, across))

    def relayed(n):
        p = RELAYED[n]
        return remote(relay.at[n], piece(xf.at[across], p), fw_s, gp_r.at[p], (0, q, m))

    def piece_in(p):
        return remote(piece(mem, p), piece(xf.at[across], p), fl_s, gp_r.at[p], (0, q, m))

    def forward(p):
        return remote(
            piece(xf.at[across], p), piece(xf.at[across], p), fw_s, gf_r.at[p], (0, q, beside)
        )

    def forward_in(p):
        there = jnp.bitwise_xor(beside, 2)
        return remote(piece(mem, p), piece(xf.at[there], p), fw_s, gf_r.at[p], (0, q, beside))

    b_mem = remote(mem, xf.at[m], gb_s, gb_r, (0, q, beside))

    def stats(to):
        return remote(st.at[m], st.at[m], st_s, st_r, (0, q, to))

    own_dec = pltpu.make_async_copy(dec, xd.at[m], own_sem)
    a_dec = remote(dec, xd.at[m], d_s.at[0], d_r.at[0], (1, q, across))
    b_dec = remote(dec, xd.at[m], d_s.at[0], d_r.at[1], (1, q, beside))
    c_dec = remote(xd.at[across], xd.at[across], d_s.at[1], d_r.at[2], (1, q, beside))

    low = lax.broadcasted_iota(jnp.int32, (1, 128), 1) < 64

    def tile_of(c, i, doc):
        return (c * SEQ + i) * 2 + doc

    def kv_out(at, i, doc):
        c, start, rows = at
        tile = kvs.at[tile_of(c, i, doc), pl.ds(start, rows)]
        return tile, kvr.at[c, q, pl.ds(start, rows)], kv_r.at[c * (1 + start // 64)]

    def unit_of(doc, i, e):
        return (0, seq_of(i), m) if doc == 0 else (1, seq_of(i), jnp.where(e % 2 == 0, m, across))

    def normalise_mem(p, h):
        at = p // 4 * 128 + p % 4 * PIECE
        for k in range(2):
            columns = pl.ds(pl.multiple_of((2 * h + k) * 1024, 1024), 1024)
            weight = gain[:, columns].astype(jnp.float32)
            for d in range(2):
                rows = slice(p * PIECE, (p + 1) * PIECE)
                part = xf[2 * h + k, d, rows, :].astype(jnp.float32)
                inverse = jnp.concatenate([inv[d, rows, :]] * 8, axis=1)
                xn[h, at + d * 64 : at + d * 64 + PIECE, k * 1024 : (k + 1) * 1024] = (
                    part * inverse * weight
                ).astype(jnp.bfloat16)

    @pl.when(encoding)
    def _():
        stats(beside).start()
        a_dec.start()
        b_mem.start()
        pltpu.make_async_copy(st.at[0:3], st.at[0:3], st_r).wait()
        for d in range(2):
            total = (st[0, d] + st[1, d]) + (st[2, d] + st[3, d])
            inverse = lax.rsqrt(total * (1.0 / 4096) + EPS)
            inv[d] = jnp.broadcast_to(inverse[0:1, :], (128, 256)).T
        tell_z()
        b_mem.wait_recv()
        for p in range(16):
            normalise_mem(p, half)
        for n in range(4):
            hop(n).start()

        def ready(p):
            forward_in(p).wait_recv()
            normalise_mem(p, 1 - half)

        def pass_beside(p):
            piece_in(p).wait_recv()
            forward(p).start()

        def rows_of(h):
            return pl.ds(pl.multiple_of(h * 2048, 2048), 2048)

        pltpu.make_async_copy(wbuf, wbuf, w_sem).wait()

        for jj in range(4):
            j = lax.rem(slot // 4 + jj, 4)
            pf[jj] = jnp.dot(xn[half], wbuf[j, rows_of(half), :], preferred_element_type=jnp.float32)
            for p in ARRIVAL[0][jj]:
                pass_beside(p)
        for p in range(4):
            ready(p)
        pl.semaphore_wait(ring_z, 3)

        def multiply(at, first, jj):
            rows = at[2]
            j = lax.rem(slot // 4 + jj, 4)
            return pf[jj, first : first + 2 * rows, :] + jnp.dot(
                xn[1 - half, first : first + 2 * rows, :],
                wbuf[j, rows_of(1 - half), :],
                preferred_element_type=jnp.float32,
            )

        def deliver(at, jj, both):
            c, start, rows = at
            j = lax.rem(slot // 4 + jj, 4)
            for u in range(2):
                key = pltpu.roll(both[:, u * 128 : (u + 1) * 128], 64, 1)
                value = both[:, 256 + u * 128 : 256 + (u + 1) * 128]
                for e in range(2):
                    i = 4 * j + 2 * u + e
                    tile = jnp.where(low, value, key) if e == 0 else jnp.where(low, key, value)
                    kvs[pl.ds(tile_of(c, i, 0), 2), start : start + rows] = tile.astype(
                        jnp.bfloat16
                    ).reshape(2, rows, 128)

            def send(e, doc):
                i = 4 * j + e
                remote(*kv_out(at, i, doc)[:2], kv_s, kv_out(at, i, doc)[2], unit_of(doc, i, e)).start()

            for k in range(4):
                e = lax.rem(z + k, 4)
                if jj + k:
                    send(e, 0)
                else:
                    pltpu.make_async_copy(*kv_out(at, slot, 0)).start()
                send(e, 1)

        for quarter in range(4):
            at, first = (quarter // 2, quarter % 2 * 64, 64), quarter * 128
            both = multiply(at, first, 0)
            for jj in range(4):
                ahead = multiply(at, first, jj + 1) if quarter == 3 and jj < 3 else None
                deliver(at, jj, both)
                if quarter < 3:
                    for p in ARRIVAL[quarter + 1][jj]:
                        pass_beside(p)
                if jj < 3:
                    both = multiply(at, first, jj + 1) if ahead is None else ahead
            if quarter == 0:
                ready(4)
                pass_beside(7)
                for p in range(5, 8):
                    ready(p)
            elif quarter < 3:
                for p in range(4 * quarter + 4, 4 * quarter + 8):
                    ready(p)

    def turned_rows(k):
        return pl.ds(pl.multiple_of(k * 1024, 1024), 1024)

    def turn(c):
        for k in range(4):
            wbuf[2 + c, turned_rows(k), :] = wo[c, k].T

    def q_out(i, doc, device):
        return remote(qs.at[i, doc], qr.at[slot], q_s, q_r, device)

    residual_out = remote(
        xd.at[m // 2, :, :, pl.ds(pl.multiple_of((m % 2) * 512, 512), 512)], res, res_s, res_r, (0, q, m)
    )

    @pl.when(decoding)
    def _():
        stats(across).start()
        stats(corner).start()
        for p in DIRECT[0]:
            direct(p).start()
        own_dec.start()
        b_dec.start()

        def pass_on(n):
            p = RELAYED[n]
            remote(piece(mem, p), relay.at[n], fl_s, gp_r.at[p], (1, q, across)).wait_recv()
            relayed(n).start()

        remote(dec, xd.at[across], d_s.at[0], d_r.at[0], (1, q, across)).wait_recv()
        c_dec.start()
        tell_z()
        own_dec.wait()
        b_dec.wait_recv()
        c_dec.wait_recv()
        for p in range(4):
            rows = slice(p * PIECE, (p + 1) * PIECE)
            total = jnp.zeros((2, PIECE, 1), jnp.float32)
            for k in range(4):
                part = xd[k, :, rows, :].astype(jnp.float32)
                total = total + jnp.sum(part * part, axis=2, keepdims=True)
            inverse = lax.rsqrt(total * (1.0 / 4096) + EPS)
            for k in range(4):
                part = xd[k, :, rows, :].astype(jnp.float32)
                wide = part * inverse * gain[:, k * 1024 : (k + 1) * 1024].astype(jnp.float32)
                wide = wide.astype(jnp.bfloat16)
                columns = slice((k % 2) * 1024, (k % 2 + 1) * 1024)
                xn[k // 2, p * PIECE : (p + 1) * PIECE, columns] = wide[0]
                xn[k // 2, 64 + p * PIECE : 64 + (p + 1) * PIECE, columns] = wide[1]
        pl.semaphore_wait(ring_z, 3)
        pass_on(0)
        pass_on(1)
        pltpu.make_async_copy(wbuf.at[0:2], wbuf.at[0:2], w_sem).wait()
        for b in range(2):
            made = jnp.dot(xn[0, :128, :], wbuf[b, :2048, :], preferred_element_type=jnp.float32)
            made = made + jnp.dot(xn[1, :128, :], wbuf[b, 2048:, :], preferred_element_type=jnp.float32)
            for u in range(4):
                pair = made[:, u * 128 : (u + 1) * 128]
                turned = pltpu.roll(pair, 64, 1)
                pair, turned = (v.reshape(2, 2, 32, 128) for v in (pair, turned))
                for e in range(2):
                    first, second = (pair, turned) if e == 0 else (turned, pair)
                    tile = jnp.where(low, first[:, 0], second[:, 1])
                    qs[2 * (4 * b + u) + e] = tile.astype(jnp.bfloat16)
        pass_on(2)
        pass_on(3)
        for jj in range(4):
            for k in range(4):
                e = lax.rem(z + k, 4)
                i = 4 * lax.rem(slot // 4 + jj, 4) + e
                q_out(i, 0, unit_of(0, i, e)).start()
                if jj + k:
                    q_out(i, 1, unit_of(1, i, e)).start()
                else:

                    @pl.when(odd == 1)
                    def _(i=i, e=e):
                        q_out(i, 1, unit_of(1, i, e)).start()

                    @pl.when(odd == 0)
                    def _():
                        pltpu.make_async_copy(qs.at[slot, 1], qr.at[slot], q_r).start()

        for p in DIRECT[1]:
            direct(p).start()
        pltpu.make_async_copy(wo.at[core], wo.at[core], wo_sem).wait()
        turn(core)

    pltpu.make_async_copy(qr, qr, q_r).wait()

    @pl.when(decoding)
    def _():
        residual_out.start()
        for k in range(4):
            o_weight_out(k).start()

    lane = lax.broadcasted_iota(jnp.int32, (1, 128), 1)
    key_half = jnp.where(odd == 1, 0, 1)
    key_lane = (lane // 64) == key_half
    packed = qr[...].astype(jnp.float32)
    turned = pltpu.roll(packed, 64, 2)
    first = jnp.where(odd == 1, packed, turned)
    second = jnp.where(odd == 1, turned, packed)
    placed = jnp.stack([first, second], axis=1).reshape(1024, 128)
    q2[...] = jnp.where(key_lane, placed, 0.0).astype(jnp.bfloat16)
    length = lens[s]
    one = jnp.bfloat16(1)
    passes = ((0, 0, 128), (1, 0, 64), (1, 64, 64))

    def keys(at):
        c, start, rows = at
        return kvr[c, :, start : start + rows, :].reshape(SEQ * rows, 128)

    def kv_wait(n):
        c, start, rows = passes[n]
        part = kvr.at[c, :, pl.ds(start, rows), :]
        pltpu.make_async_copy(part, part, kv_r.at[n]).wait()

    def score(at, rows):
        return lax.dot_general(
            q2[rows, :], keys(at), (((1,), (1,)), ((), ())), preferred_element_type=jnp.float32
        )

    def weigh(at, scores, before):
        c, start, rows = at
        column = lax.broadcasted_iota(jnp.int32, (1, SEQ * rows), 1)
        position = column // rows * 256 + c * 128 + start + column % rows
        scores = jnp.where(position < length, scores, MASKED)
        top = jnp.max(scores, axis=1, keepdims=True)
        top = jnp.broadcast_to(top, (ROWS, 128)) if before is None else jnp.maximum(before, top)
        probs = jnp.exp(scores - jnp.concatenate([top] * (SEQ * rows // 128), axis=1))
        mixed = jnp.dot(
            probs.astype(jnp.bfloat16),
            jnp.where(key_lane, one, keys(at)),
            preferred_element_type=jnp.float32,
        )
        return top, mixed

    def block(r):
        return pl.ds(pl.multiple_of(r * ROWS, ROWS), ROWS)

    blocks = 1024 // ROWS
    for n in range(2):
        kv_wait(n)
        scores = score(passes[n], block(0))
        for r in range(blocks):
            following = score(passes[n], block(r + 1)) if r + 1 < blocks else None
            before = mx[block(r), :] if n else None
            top, mixed = weigh(passes[n], scores, before)
            if n:
                mixed = acc[block(r), :] * jnp.exp(before - top) + mixed
            mx[block(r), :] = top
            acc[block(r), :] = mixed
            scores = following

    def c_out(k):
        return remote(cs.at[k], cr.at[s, slot], c_s, c_r, (1, seq_of(k), group))

    own_context = jnp.logical_and(decoding, odd == 0)

    kv_wait(2)
    order = [lax.rem(slot // 4 + r, blocks) for r in range(blocks)]

    def finish(n, mixed):
        r = order[n]
        context = mixed / pltpu.roll(mixed, 64, 1)
        context = jnp.where(key_lane, pltpu.roll(context, 64, 1), context).reshape(4, 2, 32, 128)
        cs[pl.ds(r * 4, 4)] = jnp.where(low, context[:, 0], context[:, 1]).astype(jnp.bfloat16)
        for k in range(4):
            to = 4 * r + lax.rem(z + k, 4)
            if n + k:
                c_out(to).start()
            else:

                @pl.when(jnp.logical_not(own_context))
                def _(to=to):
                    c_out(to).start()

                @pl.when(own_context)
                def _():
                    pltpu.make_async_copy(cs.at[slot], cr.at[1, slot], c_r).start()

    scores = score(passes[2], block(order[0]))
    mixed = None
    for n, r in enumerate(order):
        following = score(passes[2], block(order[n + 1])) if n + 1 < blocks else None
        before = mx[block(r), :]
        top, added = weigh(passes[2], scores, before)
        added = acc[block(r), :] * jnp.exp(before - top) + added
        if n:
            finish(n - 1, mixed)
        mixed, scores = added, following
    finish(blocks - 1, mixed)

    def x_out(c):
        return remote(cx.at[c], cx.at[c], x_s, x_r, (1, q, beside))

    def rs_out(k):
        return remote(rs.at[k], rr.at[half], rs_s, rs_r, (k // 2, q, 2 * (k % 2) + core))

    @pl.when(decoding)
    def _():
        remote(wo.at[core], wo.at[1 - core], wx_s, wx_r, (1, q, beside)).wait_recv()
        turn(1 - core)
        pltpu.make_async_copy(cr, cr, c_r).wait()
        for d in range(2):
            for t in range(8):
                first = cr[d, 2 * t].astype(jnp.float32)
                second = cr[d, 2 * t + 1].astype(jnp.float32)
                at = slice(t * 128, (t + 1) * 128)
                upper = jnp.where(low, first, pltpu.roll(second, 64, 1))
                lower = jnp.where(low, pltpu.roll(first, 64, 1), second)
                cx[core, d * 64 : d * 64 + 32, at] = upper.astype(jnp.bfloat16)
                cx[core, d * 64 + 32 : d * 64 + 64, at] = lower.astype(jnp.bfloat16)
        x_out(core).start()

        def partial(c, k):
            return jnp.dot(cx[c], wbuf[2 + c, turned_rows(k), :], preferred_element_type=jnp.float32)

        far, own = 3 - half, 2 + half
        for k in (0, far, 1, own):
            po[k] = partial(core, k)
        x_out(1 - core).wait_recv()
        for k in (0, far, 1):
            part = po[k] + partial(1 - core, k)
            rs[k] = part.astype(jnp.bfloat16).reshape(2, 64, 512)
            rs_out(k).start()
        part = po[own] + partial(1 - core, own)
        rr[half] = part.astype(jnp.bfloat16).reshape(2, 64, 512)
        res[...] = xd[2 + half, :, :, pl.ds(pl.multiple_of(core * 512, 512), 512)]

    @pl.when(encoding)
    def _():
        residual_out.wait_recv()

    @pl.when(encoding)
    def _():
        pltpu.make_async_copy(rr, rr, rs_r).wait()

    @pl.when(decoding)
    def _():
        pltpu.make_async_copy(rr.at[0], rr.at[0], rs_r).wait()

    update = rr[0].astype(jnp.float32) + rr[1].astype(jnp.float32)
    out[...] = (res[...].astype(jnp.float32) + update).astype(jnp.bfloat16)

    def sent(ref, sem):
        remote(ref, ref, sem, sem, (s, q, m)).wait_send()

    @pl.when(jnp.logical_not(own_context))
    def _():
        sent(cs, c_s)

    @pl.when(own_context)
    def _():
        sent(cs.at[0:15], c_s)

    @pl.when(encoding)
    def _():
        a_dec.wait_send()
        sent(relay, fl_s)
        sent(xf.at[0], fw_s)
        b_mem.wait_send()
        sent(st.at[0], st_s)
        sent(kvs.at[0:62], kv_s)

    @pl.when(decoding)
    def _():
        sent(relay, fw_s)
        sent(st.at[0:2], st_s)
        sent(xf.at[0, :, 0:192, :], fl_s)
        b_dec.wait_send()
        c_dec.wait_send()
        residual_out.wait_send()
        x_out(core).wait_send()
        sent(wo.at[core], wx_s)

        @pl.when(odd == 1)
        def _():
            sent(qs, q_s)

        @pl.when(odd == 0)
        def _():
            sent(acc.at[0:496], q_s)

        sent(rs.at[0:3], rs_s)


def on_device(memory, decoder_rows, gains, weights, lengths):
    bf16, f32 = jnp.bfloat16, jnp.float32
    anywhere = pl.BlockSpec(memory_space=pl.ANY)
    vmem = pl.BlockSpec(memory_space=pltpu.VMEM)
    dma = pltpu.SemaphoreType.DMA
    return pl.pallas_call(
        body,
        name="cross_attention",
        out_shape=jax.ShapeDtypeStruct((2, 64, 512), bf16),
        in_specs=[anywhere, anywhere, vmem, anywhere, pl.BlockSpec(memory_space=pltpu.SMEM)],
        out_specs=vmem,
        scratch_shapes=[
            pltpu.VMEM((4, 4096, 512), bf16),
            pltpu.VMEM((2, 4, 512, 1024), bf16),
            pltpu.VMEM((4, 2, 256, 1024), bf16),
            pltpu.VMEM((4, 2, 64, 1024), bf16),
            pltpu.VMEM((4, 2, PIECE, 1024), bf16),
            pltpu.VMEM((256, 128), f32),
            pltpu.VMEM((4, 2, 8, 256), f32),
            pltpu.VMEM((2, 256, 128), f32),
            pltpu.VMEM((2, 512, 2048), bf16),
            pltpu.VMEM((4, 512, 512), f32),
            pltpu.VMEM((4, 128, 512), f32),
            pltpu.VMEM((64, 128, 128), bf16),
            pltpu.VMEM((2, 16, 128, 128), bf16),
            pltpu.VMEM((16, 2, 32, 128), bf16),
            pltpu.VMEM((16, 32, 128), bf16),
            pltpu.VMEM((1024, 128), bf16),
            pltpu.VMEM((1024, 128), f32),
            pltpu.VMEM((1024, 128), f32),
            pltpu.VMEM((16, 32, 128), bf16),
            pltpu.VMEM((2, 16, 32, 128), bf16),
            pltpu.VMEM((2, 128, 1024), bf16),
            pltpu.VMEM((4, 2, 64, 512), bf16),
            pltpu.VMEM((2, 2, 64, 512), bf16),
            pltpu.VMEM((2, 64, 512), bf16),
            dma,
            dma,
            dma,
            dma,
            dma,
            dma((16,)),
            dma((16,)),
            dma,
            dma,
            dma,
            dma,
            dma,
            dma,
            dma((2,)),
            dma((3,)),
            dma,
            dma((3,)),
            dma,
            dma,
            dma,
            dma,
            dma,
            dma,
            dma,
            dma,
            dma,
            dma,
            pltpu.SemaphoreType.REGULAR,
            pltpu.SemaphoreType.REGULAR,
        ],
        compiler_params=pltpu.CompilerParams(
            collective_id=0, has_side_effects=True, vmem_limit_bytes=60 << 20
        ),
    )(memory, decoder_rows, gains, weights, lengths)


def solution(mesh):
    in_specs = (
        P(None, "seq", "mp"),
        P(None, "seq", "mp"),
        P("segment", None),
        P("segment", None, None, "mp"),
        P(),
    )
    out_specs = P(None, "seq", ("segment", "mp"))
    return jax.shard_map(
        on_device, mesh=mesh, in_specs=in_specs, out_specs=out_specs, check_vma=False
    )
```
